256 devices in a mesh: sec: 16 (over x, z_lo, core), ty: 4 (over y), tx: 4 (over z_hi).
Axes of the slice: x: 4, y: 4, z: 8 (z_hi: 4, z_lo: 2; z = z_hi * 2 + z_lo), core: 2. Of those that a mesh axis runs over, the one named last changes fastest.
Arguments:
- descriptors: bfloat16 [16, 4, 4, 1024, 128], P('sec', 'ty', 'tx'), may hold values from -4 to 4, as said below
- positions: bfloat16 [16, 4, 4, 2, 1024], P('sec', 'ty', 'tx'), may hold values from -1 to 1
- vertex_ids: int32 [16, 4, 4, 1024], P('sec', 'ty', 'tx'), may hold values from 0 to 262143, as said below
- candidate_blocks: int32 [16, 4, 4, 32], P('sec', 'ty', 'tx'), may hold values from 0 to 127, as said below
- candidate_count: int32 [16, 4, 4], P('sec', 'ty', 'tx'), may hold values from 8 to 32, as said below
- displacement: float32 [16, 2, 512, 512], P('sec', None, 'ty', 'tx'), may hold values from -3 to 3
- stiffness: float32 [16, 512, 512], P('sec', 'ty', 'tx'), may hold values from 0.25 to 4
Outputs:
- relaxed: float32 [16, 2, 512, 512], P('sec', None, 'ty', 'tx')
The draws below stay inside these ranges and needn't reach their ends.
Inputs may be any that keep to these rules, and one draw needn't show every extreme that they name: `descriptors`: descriptor entries stay within the range. `candidate_blocks`: A list names distinct blocks tile * 8 + j of the next section; among its live entries at most 4 blocks come from any one tile, and some list has 4 live blocks of one tile. `candidate_count`: some tile has all 32 entries live. `vertex_ids`: ids follow the vertex numbering of the steps, anywhere in the section.
All inputs are finite; a program needn't handle non-finite values.
Results may differ from the reference program's by a relative error of at most 0.0019.
Values may be sent and summed in bfloat16 or wider, within the bound.
A program may use at most 192 MiB of HBM per device.

```python
import math
import jax
import jax.numpy as jnp
from jax import lax

DESC = 128
PTS = 1024
BLK = 128
CAND = 32
MV = 128
ITERS = 4
NS = 16
TILE_ROWS = 4
TILE_COLS = 4
NTILE = 16
NB = 8
CAPB = 4
NYV = 512
NXV = 512


def first_blocks(block_key):
    return jax.random.permutation(block_key, NB)[:CAPB]


def one_list(list_key):
    order_key, block_key, mix_key = jax.random.split(list_key, 3)
    tile_order = jax.random.permutation(order_key, NTILE)
    chosen_blocks = jax.vmap(first_blocks)(jax.random.split(block_key, NTILE))
    block_pool = (tile_order[:, None] * NB + chosen_blocks[tile_order]).reshape(-1)
    picked = block_pool[:CAND]
    return picked[jax.random.permutation(mix_key, CAND)]


def candidate_lists(base_key):
    list_total = NS * NTILE
    all_lists = jax.vmap(one_list)(jax.random.split(jax.random.fold_in(base_key, 1), list_total))
    counts = jax.random.randint(jax.random.fold_in(base_key, 2), (list_total,), max(1, CAND // 4), CAND + 1)
    counts = counts.at[0].set(CAND)
    return (all_lists.reshape(NS, TILE_ROWS, TILE_COLS, CAND).astype(jnp.int32), counts.reshape(NS, TILE_ROWS, TILE_COLS).astype(jnp.int32))


def draw_candidate_blocks(key, part):
    return candidate_lists(jax.random.fold_in(key, 7))[0]


def draw_candidate_count(key, part):
    return candidate_lists(jax.random.fold_in(key, 7))[1]


def draw_vertex_ids(key, part):
    shape = (NS, TILE_ROWS, TILE_COLS, PTS)
    own_key, other_key, pick_key = jax.random.split(jax.random.fold_in(key, 5), 3)
    tile_base = (jnp.arange(NTILE, dtype=jnp.int32) * (MV * MV)).reshape(1, TILE_ROWS, TILE_COLS, 1)
    own_vertex = tile_base + jax.random.randint(own_key, shape, 0, MV * MV)
    other_vertex = jax.random.randint(other_key, shape, 0, NTILE * MV * MV)
    chosen = jax.random.randint(pick_key, shape, 0, 4) == 0
    vertex = jnp.where(chosen, other_vertex, own_vertex)
    vertex = vertex.at[0, 0, 0, 0].set(NTILE * MV * MV - 1)
    return vertex.astype(jnp.int32)


def draw_descriptors(key, part):
    shape = (NS, NTILE, PTS, DESC)
    base_key = jax.random.fold_in(key, 11)
    entries = jax.random.truncated_normal(base_key, -4.0, 4.0, shape, jnp.float32)
    return entries.reshape(NS, TILE_ROWS, TILE_COLS, PTS, DESC).astype(jnp.bfloat16)


def level_of(key, shape, pieces, least, top_value):
    def one(axis_at, parts):
        heights = jax.random.uniform(jax.random.fold_in(jax.random.fold_in(key, 6), axis_at), (parts,), jnp.float32, least / len(pieces), top_value / len(pieces))
        return jnp.repeat(jnp.exp(heights), shape[axis_at] // parts).reshape((-1,) + (1,) * (len(shape) - axis_at - 1))

    gain = one(*pieces[0])
    for cut in pieces[1:]:
        gain = gain * one(*cut)
    return gain


def noise(key, shape, deviation, most, cuts=(), held_as=jnp.bfloat16):
    values = deviation * jax.random.normal(key, shape, jnp.float32)
    if cuts:
        values = values * level_of(key, shape, cuts, -0.22, 0.18)
    return jnp.clip(values, -most, most).astype(held_as)


def setup_inputs(seed: int = 0) -> dict:
    arg_keys = jax.random.split(jax.random.key(seed), 8)
    descriptors = draw_descriptors(jax.random.fold_in(arg_keys[7], 71), 0)
    positions = jnp.clip(jax.random.uniform(arg_keys[1], (NS, TILE_ROWS, TILE_COLS, 2, PTS), jnp.float32, -1.0, 1.0) * level_of(arg_keys[1], (NS, TILE_ROWS, TILE_COLS, 2, PTS), ((0, 16), (1, 4), (2, 4)), -0.4, 0.0), -1.0, 1.0).astype(jnp.bfloat16)
    vertex_ids = draw_vertex_ids(jax.random.fold_in(arg_keys[7], 71), 0)
    candidate_blocks = draw_candidate_blocks(jax.random.fold_in(arg_keys[7], 71), 0)
    candidate_count = draw_candidate_count(jax.random.fold_in(arg_keys[7], 71), 0)
    displacement = noise(arg_keys[5], (NS, 2, NYV, NXV), 0.5, 3.0, ((0, 16), (2, 4), (3, 4)), jnp.float32)
    stiffness = jnp.clip(jnp.exp(math.log(4.0) - 2.7725887 * jax.random.uniform(arg_keys[6], (NS, NYV, NXV), jnp.float32) ** level_of(arg_keys[6], (NS, NYV, NXV), ((0, 16), (1, 4), (2, 4)), -0.2, 0.2)), 0.25, 4.0)
    return {"descriptors": descriptors, "positions": positions, "vertex_ids": vertex_ids, "candidate_blocks": candidate_blocks, "candidate_count": candidate_count, "displacement": displacement, "stiffness": stiffness}


def reference(descriptors, positions, vertex_ids, candidate_blocks, candidate_count, displacement, stiffness):
    spring_sec = 0.5
    spring_match = 1.0
    relax_rate = 0.8
    score_factor = 16.0 / DESC
    desc_all = descriptors.reshape(NS, NTILE, PTS, DESC)
    place_all = positions.reshape(NS, NTILE, 2, PTS).astype(jnp.float32)
    list_all = candidate_blocks.reshape(NS * NTILE, CAND)
    live_all = candidate_count.reshape(NS * NTILE)

    def match_tile(list_index):
        section = list_index // NTILE
        tile_index = list_index % NTILE
        following = jnp.minimum(section + 1, NS - 1)
        queries = desc_all[section, tile_index]
        next_plane = desc_all[following].reshape(NTILE * NB, BLK, DESC)
        plane_place = place_all[following].reshape(NTILE, 2, NB, BLK).transpose(0, 2, 1, 3).reshape(NTILE * NB, 2, BLK)
        block_list = list_all[list_index]
        key_rows = next_plane[block_list].reshape(CAND * BLK, DESC)
        key_place = plane_place[block_list].transpose(1, 0, 2).reshape(2, CAND * BLK)
        is_live = jnp.repeat(jnp.arange(CAND) < live_all[list_index], BLK)
        scores = jnp.dot(queries, key_rows.T, preferred_element_type=jnp.float32) * score_factor
        masked = jnp.where(is_live[None, :], scores, -1e30)
        row_top = jnp.max(masked, axis=1)
        weights = jnp.where(is_live[None, :], jnp.exp(masked - row_top[:, None]), 0.0)
        denominator = jnp.sum(weights, axis=1)
        target = jnp.einsum("ck,qk->cq", key_place, weights, precision=lax.Precision.HIGHEST) / denominator[None, :]
        has_next = (section < NS - 1).astype(jnp.float32)
        pull_vec = (target - place_all[section, tile_index]) * has_next
        return jnp.concatenate([pull_vec, jnp.broadcast_to(has_next, (1, PTS)).astype(jnp.float32)], axis=0)

    pulls = lax.map(match_tile, jnp.arange(NS * NTILE, dtype=jnp.int32))
    vertex = vertex_ids.reshape(NS * NTILE, PTS)
    tile_of = vertex // (MV * MV)
    within = vertex % (MV * MV)
    grid_row = (tile_of // TILE_COLS) * MV + within // MV
    grid_col = (tile_of % TILE_COLS) * MV + within % MV
    sec_of = jnp.broadcast_to((jnp.arange(NS * NTILE, dtype=jnp.int32) // NTILE)[:, None], vertex.shape)
    sums = jnp.zeros((NS, 3, NYV, NXV), jnp.float32)
    for channel in range(3):
        sums = sums.at[sec_of, channel, grid_row, grid_col].add(pulls[:, channel, :])
    pulled = sums[:, 0:2]
    matched = sums[:, 2][:, None]
    linked = ((jnp.arange(NS) > 0).astype(jnp.float32) + (jnp.arange(NS) < NS - 1).astype(jnp.float32))[:, None, None, None]
    gains = stiffness[:, None]
    moving = displacement
    for sweep in range(ITERS):
        padded = jnp.pad(moving, ((0, 0), (0, 0), (1, 1), (1, 1)))
        laplace = padded[:, :, 2:, 1:-1] + padded[:, :, :-2, 1:-1] + padded[:, :, 1:-1, 2:] + padded[:, :, 1:-1, :-2] - 4.0 * moving
        lower_sec = jnp.concatenate([jnp.zeros_like(moving[:1]), moving[:-1]], axis=0)
        upper_sec = jnp.concatenate([moving[1:], jnp.zeros_like(moving[:1])], axis=0)
        spring_force = gains * laplace + spring_sec * (lower_sec + upper_sec - linked * moving) + spring_match * (pulled - matched * moving)
        diagonal = 4.0 * gains + spring_sec * linked + spring_match * matched
        moving = moving + relax_rate * spring_force / diagonal
    return moving
```

```python
import functools
import math

import jax
import jax.numpy as jnp
from jax import lax
from jax.experimental import pallas as pl
from jax.experimental.pallas import tpu as pltpu
from jax.sharding import PartitionSpec as P

MESH = pl.DeviceIdType.MESH
BLK = 128
CAPB = 4
ITERS = 4
NEG = -1e30
SPRING_SEC = 0.5
RATE = 0.8
NT = (((1,), (1,)), ((), ()))
NN = (((1,), (0,)), ((), ()))


def remote(src, dst, send, recv, device):
    return pltpu.make_async_remote_copy(
        src_ref=src, dst_ref=dst, send_sem=send, recv_sem=recv, device_id=device, device_id_type=MESH
    )


def block_table(list_ref, count_ref, slots):
    lane = lax.broadcasted_iota(jnp.int32, (8, 128), 1)
    row = lax.broadcasted_iota(jnp.int32, (8, 128), 0)
    within = lane & 7
    wanted = jnp.zeros((8, 128), jnp.int32)
    for entry in range(slots):
        block = jnp.where(count_ref[0] > entry, list_ref[entry], -1)
        wanted = jnp.where(lane == block, 1, wanted)
    rank = jnp.zeros((8, 128), jnp.int32)
    for by in range(1, 8):
        rank = rank + jnp.where(within >= by, pltpu.roll(wanted, by, 1), 0)
    picked = jnp.where((wanted == 1) & (rank == row), within + 1, 0)
    total = picked
    for by in range(1, 8):
        total = total + pltpu.roll(picked, 128 - by, 1)
    return jnp.where(total == 0, 8, total - 1)


def kernel(
    sizes, list_ref, count_ref, desc, pos, ids, disp, stiff, out,
    qbuf, kin0, kin1, kin2, kin3, pin, kwork, vwork, tabv, tabs, idb, onea, onec, mcount,
    acc, mx, part, prt, pull, pbuf, scat, ub, lob, upb, edge, halo,
    qs, qr, hs, hr, ks, kr, ts, tr, tl, ids_s, ids_r, ps, pr, cs, cr, us, ur,
):
    ns, ny, nz, slots = sizes
    plane = ny * nz
    pts, feat = desc.shape
    half = pts // 2
    blocks = pts // BLK
    side = stiff.shape[0]
    s, y, z = lax.axis_index("sec"), lax.axis_index("ty"), lax.axis_index("tx")
    me = y * nz + z
    right, left = {"tx": lax.rem(z + 1, nz)}, {"tx": lax.rem(z + nz - 1, nz)}
    across = {"tx": lax.rem(z + 2, nz)}
    down, up = {"ty": lax.rem(y + 1, ny)}, {"ty": lax.rem(y + ny - 1, ny)}
    after, before = {"sec": lax.rem(s + 1, ns)}, {"sec": lax.rem(s + ns - 1, ns)}

    def peer(by):
        tile = lax.rem(me + by, plane)
        return tile, {"ty": lax.div(tile, nz), "tx": lax.rem(tile, nz)}

    barrier = pltpu.get_barrier_semaphore()

    def greet(by, carry):
        pl.semaphore_signal(barrier, inc=1, device_id=peer(by)[1], device_id_type=MESH)
        return carry

    lax.fori_loop(1, plane, greet, 0)
    for device in (after, before):
        pl.semaphore_signal(barrier, inc=1, device_id=device, device_id_type=MESH)

    tabv[0] = block_table(list_ref, count_ref, slots)
    qbuf[0] = desc[...]
    idb[pl.ds(me, 1)] = ids[...][None]
    acc[...] = jnp.zeros_like(acc)
    mx[...] = jnp.full_like(mx, NEG)
    mcount[...] = jnp.zeros_like(mcount)
    scat[...] = jnp.zeros_like(scat)

    pl.semaphore_wait(barrier, plane + 1)

    rows = [pl.ds(0, half), pl.ds(half, half)]
    shift = [
        remote(desc.at[rows[0]], kin0.at[rows[0]], hs.at[0], hr.at[0], before),
        remote(desc.at[rows[1]], kin0.at[rows[1]], hs.at[1], hr.at[1], before),
        remote(pos, pin.at[0], hs.at[2], hr.at[2], before),
    ]
    tables = [
        remote(tabv.at[0], tabv.at[1], ts.at[0], tr.at[0], right),
        remote(tabv.at[0], tabv.at[2], ts.at[1], tr.at[1], left),
        remote(tabv.at[0], tabv.at[3], ts.at[2], tr.at[2], across),
    ]
    queries = [
        remote(desc.at[rows[0]], qbuf.at[1, rows[0]], qs.at[0], qr.at[0], right),
        remote(desc.at[rows[1]], qbuf.at[2, rows[1]], qs.at[1], qr.at[1], left),
        remote(desc.at[rows[1]], qbuf.at[1, rows[1]], qs.at[2], qr.at[2], right),
        remote(desc.at[rows[0]], qbuf.at[2, rows[0]], qs.at[3], qr.at[3], left),
        remote(qbuf.at[1, rows[0]], qbuf.at[3, rows[0]], qs.at[4], qr.at[4], right),
        remote(qbuf.at[2, rows[1]], qbuf.at[3, rows[1]], qs.at[5], qr.at[5], left),
    ]
    keys = [
        remote(kin0.at[rows[0]], kin1.at[rows[0]], ks.at[0], kr.at[0], down),
        remote(kin0.at[rows[1]], kin2.at[rows[1]], ks.at[1], kr.at[1], up),
        remote(kin0.at[rows[1]], kin1.at[rows[1]], ks.at[2], kr.at[2], down),
        remote(kin0.at[rows[0]], kin2.at[rows[0]], ks.at[3], kr.at[3], up),
        remote(kin1.at[rows[0]], kin3.at[rows[0]], ks.at[4], kr.at[4], down),
        remote(kin2.at[rows[1]], kin3.at[rows[1]], ks.at[5], kr.at[5], up),
        remote(pin.at[0], pin.at[1], ks.at[6], kr.at[6], down),
        remote(pin.at[0], pin.at[2], ks.at[7], kr.at[7], up),
        remote(pin.at[1], pin.at[3], ks.at[8], kr.at[8], down),
    ]
    partials = [
        remote(part.at[1], prt.at[2], cs.at[0], cr.at[0], left),
        remote(part.at[2], prt.at[1], cs.at[1], cr.at[1], right),
        remote(part.at[3], prt.at[3], cs.at[2], cr.at[2], across),
    ]

    def exchange(turn):
        source = disp if turn == 0 else ub.at[turn - 1]
        return [
            remote(edge.at[turn, 0], halo.at[turn, 1], us.at[turn, 0], ur.at[turn, 0], up),
            remote(edge.at[turn, 1], halo.at[turn, 0], us.at[turn, 1], ur.at[turn, 1], down),
            remote(edge.at[turn, 2], halo.at[turn, 3], us.at[turn, 2], ur.at[turn, 2], left),
            remote(edge.at[turn, 3], halo.at[turn, 2], us.at[turn, 3], ur.at[turn, 3], right),
            remote(source, lob.at[turn], us.at[turn, 4], ur.at[turn, 4], after),
            remote(source, upb.at[turn], us.at[turn, 5], ur.at[turn, 5], before),
        ]

    swaps = [exchange(turn) for turn in range(ITERS)]

    def ids_copy(by):
        _, device = peer(by)
        return remote(idb.at[me], idb.at[me], ids_s.at[by], ids_r.at[me], device)

    def ids_from(tile):
        return remote(idb.at[tile], idb.at[tile], ids_s.at[0], ids_r.at[tile], before)

    def pull_copy(by):
        _, device = peer(by)
        return remote(pull, pbuf.at[me], ps.at[by], pr.at[me], device)

    def pull_from(tile):
        return remote(pull, pbuf.at[tile], ps.at[0], pr.at[tile], before)

    def start_ids(by, carry):
        ids_copy(by).start()
        return carry

    for copy in shift[:2]:
        copy.start()
    for copy in tables:
        copy.start()
    for copy in queries[:4]:
        copy.start()
    shift[2].start()
    lax.fori_loop(1, plane, start_ids, 0)

    def set_key(slot, source):
        kwork[slot] = source[...].reshape(blocks, BLK, feat)
        place = pin[slot].astype(jnp.float32)
        line = lax.broadcasted_iota(jnp.int32, (16, pts), 0)
        value = jnp.where(line == 2, 1.0, 0.0)
        value = jnp.where(line == 1, place[1:2], value)
        value = jnp.where(line == 0, place[0:1], value).astype(jnp.bfloat16)
        for block in range(blocks):
            vwork[slot, block] = value[:, block * BLK : (block + 1) * BLK]

    eye = lax.broadcasted_iota(jnp.int32, (side, side), 0) == lax.broadcasted_iota(jnp.int32, (side, side), 1)

    def set_edges(turn, channel, value):
        edge[turn, 0, channel : channel + 1, :] = value[0:1, :]
        edge[turn, 1, channel : channel + 1, :] = value[side - 1 : side, :]
        for at, column in ((2, value[:, 0:1]), (3, value[:, side - 1 : side])):
            spread = jnp.where(eye, jnp.broadcast_to(column, (side, side)), 0.0)
            edge[turn, at, channel : channel + 1, :] = jnp.sum(spread, axis=0, keepdims=True)

    for channel in range(2):
        set_edges(0, channel, disp[channel])

    def one_hots(by, carry):
        tile, _ = peer(by)

        @pl.when(by > 0)
        def _():
            ids_from(tile).wait_recv()

        vertex = idb[tile]
        level = lax.broadcasted_iota(jnp.int32, (side, pts), 0)
        pick_row = level == ((vertex - me * (side * side)) >> 7)
        pick_col = level == (vertex & (side - 1))
        row_hot = jnp.where(pick_row, 1.0, 0.0).astype(jnp.bfloat16)
        col_hot = jnp.where(pick_col, 1.0, 0.0).astype(jnp.bfloat16)
        onea[tile] = row_hot
        onec[tile] = col_hot
        mcount[...] += lax.dot_general(row_hot, col_hot, NT, preferred_element_type=jnp.float32)
        return carry

    factor = 16.0 / feat * math.log2(math.e)
    chunk = 256

    def match(step, carry):
        q, k = lax.div(step, 4), lax.rem(step, 4)

        @pl.when(step == 1)
        def _():
            queries[0].wait_recv()
            queries[4].start()
            queries[1].wait_recv()
            queries[5].start()
            keys[0].wait_recv()
            keys[4].start()
            keys[1].wait_recv()
            keys[5].start()
            keys[6].wait_recv()
            keys[8].start()
            lax.fori_loop(0, plane, one_hots, 0)
            keys[2].wait_recv()
            set_key(1, kin1)

        @pl.when(step == 2)
        def _():
            keys[3].wait_recv()
            keys[7].wait_recv()
            set_key(2, kin2)

        @pl.when(step == 3)
        def _():
            keys[4].wait_recv()
            keys[5].wait_recv()
            keys[8].wait_recv()
            set_key(3, kin3)

        for slot in range(1, 4):

            @pl.when(step == 4 * slot)
            def _():
                for copy in ((), (2,), (3,), (4, 5))[slot]:
                    queries[copy].wait_recv()
                tables[slot - 1].wait_recv()
                local = pltpu.make_async_copy(tabv.at[slot], tabs.at[slot], tl.at[slot])
                local.start()
                local.wait()

        @pl.when(step == 12)
        def _():
            for copy in swaps[0]:
                copy.start()

        key_row = lax.rem(y + jnp.where(k == 1, ny - 1, jnp.where(k == 2, 1, jnp.where(k == 3, 2, 0))), ny)
        lane = (key_row * nz + z) * 8
        codes = [tabs[q, slot, lane] for slot in range(CAPB)]
        found = [code & (blocks - 1) for code in codes]
        biases = [jnp.where(code < blocks, 0.0, NEG) for code in codes]
        key_rows = jnp.concatenate([kwork[k, block] for block in found], axis=0)
        values = jnp.concatenate([vwork[k, block] for block in found], axis=1)
        for at in range(pts // chunk):
            cols = pl.ds(at * chunk, chunk)
            scores = lax.dot_general(key_rows, qbuf[q, cols, :], NT, preferred_element_type=jnp.float32)
            scores = jnp.concatenate(
                [scores[i * BLK : (i + 1) * BLK] * factor + biases[i] for i in range(CAPB)], axis=0
            )
            old = mx[q, :, cols]
            new = jnp.maximum(old, jnp.max(scores, axis=0, keepdims=True))
            weights = jnp.exp2(scores - new).astype(jnp.bfloat16)
            added = lax.dot_general(values, weights, NN, preferred_element_type=jnp.float32)
            acc[q, :, cols] = acc[q, :, cols] * jnp.exp2(old - new) + added
            mx[q, :, cols] = new

        @pl.when(k == 3)
        def _():
            part[q, 0:3, :] = acc[q, 0:3, :]
            part[q, 3:4, :] = mx[q]

        for slot in range(1, 4):

            @pl.when(step == 4 * slot + 3)
            def _():
                partials[slot - 1].start()

        return carry

    local = pltpu.make_async_copy(tabv.at[0], tabs.at[0], tl.at[0])
    local.start()
    local.wait()
    shift[0].wait_recv()
    keys[0].start()
    shift[1].wait_recv()
    keys[1].start()
    keys[2].start()
    keys[3].start()
    shift[2].wait_recv()
    keys[6].start()
    keys[7].start()
    set_key(0, kin0)
    lax.fori_loop(0, 16, match, 0)

    has_next = s < ns - 1
    for copy in partials:
        copy.wait_recv()
    pieces = [part[0]] + [prt[slot] for slot in range(1, 4)]
    top = functools.reduce(jnp.maximum, [piece[3:4] for piece in pieces])
    scaled = [piece[0:3] * jnp.exp2(piece[3:4] - top) for piece in pieces]
    total = functools.reduce(jnp.add, scaled)
    mine = pos[...].astype(jnp.float32)
    pull[...] = jnp.where(has_next, total[0:2] / total[2:3] - mine, 0.0)

    def start_pull(by, carry):
        pull_copy(by).start()
        return carry

    lax.fori_loop(1, plane, start_pull, 0)
    pbuf[pl.ds(me, 1)] = pull[...][None]

    def gather_pull(by, carry):
        tile, _ = peer(by)

        @pl.when(by > 0)
        def _():
            pull_from(tile).wait_recv()

        row_hot = onea[tile].reshape(side // 16, 16, pts)
        pieces = []
        for channel in range(2):
            value = jnp.broadcast_to(pbuf[tile, channel : channel + 1, :], (16, pts))
            high = value.astype(jnp.bfloat16)
            low = (value - high.astype(jnp.float32)).astype(jnp.bfloat16)
            for piece in (high, low):
                pieces.append((row_hot * piece[None]).reshape(side, pts))
        stacked = jnp.concatenate(pieces, axis=0)
        scat[...] += lax.dot_general(stacked, onec[tile], NT, preferred_element_type=jnp.float32)
        return carry

    lax.fori_loop(0, plane, gather_pull, 0)

    flag = lambda test: jnp.where(test, 1.0, 0.0)
    next_flag, last_flag = flag(s < ns - 1), flag(s > 0)
    linked = next_flag + last_flag
    matched = mcount[...] * next_flag
    gains = stiff[...]
    inverse = RATE / (4.0 * gains + SPRING_SEC * linked + matched)
    pulled = [scat[0:side] + scat[side : 2 * side], scat[2 * side : 3 * side] + scat[3 * side :]]
    row_at = lax.broadcasted_iota(jnp.int32, (side, side), 0)
    col_at = lax.broadcasted_iota(jnp.int32, (side, side), 1)
    flags = [flag(y > 0), flag(y < ny - 1), flag(z > 0), flag(z < nz - 1)]

    for turn in range(ITERS):
        for copy in swaps[turn]:
            copy.wait_recv()
        for channel in range(2):
            value = disp[channel] if turn == 0 else ub[turn - 1, channel]
            lines = [halo[turn, at, channel : channel + 1, :] * flags[at] for at in range(4)]
            cols = [
                jnp.sum(jnp.where(eye, jnp.broadcast_to(line, (side, side)), 0.0), axis=1, keepdims=True)
                for line in lines[2:]
            ]
            around = jnp.where(row_at == 0, lines[0], pltpu.roll(value, 1, 0))
            around += jnp.where(row_at == side - 1, lines[1], pltpu.roll(value, side - 1, 0))
            around += jnp.where(col_at == 0, cols[0], pltpu.roll(value, 1, 1))
            around += jnp.where(col_at == side - 1, cols[1], pltpu.roll(value, side - 1, 1))
            force = gains * (around - 4.0 * value) + pulled[channel] - matched * value
            force += SPRING_SEC * (
                lob[turn, channel] * last_flag + upb[turn, channel] * next_flag - linked * value
            )
            moved = value + force * inverse
            if turn == ITERS - 1:
                out[channel] = moved
            else:
                ub[turn, channel] = moved
                set_edges(turn + 1, channel, moved)
        if turn < ITERS - 1:
            for copy in swaps[turn + 1]:
                copy.start()

    for copy in shift + tables + queries + keys + partials + [c for swap in swaps for c in swap]:
        copy.wait_send()

    def finish(by, carry):
        ids_copy(by).wait_send()
        pull_copy(by).wait_send()
        return carry

    lax.fori_loop(1, plane, finish, 0)


def solution(mesh):
    ns, ny, nz = mesh.shape["sec"], mesh.shape["ty"], mesh.shape["tx"]

    def per_device(desc, pos, ids, blocks, count, disp, stiff):
        desc, pos, ids = desc[0, 0, 0], pos[0, 0, 0], ids[0, 0]
        blocks, count = blocks[0, 0, 0], count.reshape(1)
        disp, stiff = disp[0], stiff[0]
        pts, feat = desc.shape
        side = stiff.shape[0]
        plane = ny * nz
        bf16, f32, i32 = jnp.bfloat16, jnp.float32, jnp.int32
        tile = pltpu.VMEM((pts, feat), bf16)
        dma = pltpu.SemaphoreType.DMA
        smem = pl.BlockSpec(memory_space=pltpu.SMEM)
        vmem = pl.BlockSpec(memory_space=pltpu.VMEM)
        moved = pl.pallas_call(
            functools.partial(kernel, (ns, ny, nz, blocks.shape[0])),
            out_shape=jax.ShapeDtypeStruct(disp.shape, f32),
            in_specs=[smem, smem] + [vmem] * 5,
            out_specs=vmem,
            scratch_shapes=[
                pltpu.VMEM((4, pts, feat), bf16),
                tile, tile, tile, tile,
                pltpu.VMEM((4, 2, pts), bf16),
                pltpu.VMEM((4, pts // BLK, BLK, feat), bf16),
                pltpu.VMEM((4, pts // BLK, 16, BLK), bf16),
                pltpu.VMEM((4, 8, 128), i32),
                pltpu.SMEM((4, 8, 128), i32),
                pltpu.VMEM((plane, 1, pts), i32),
                pltpu.VMEM((plane, side, pts), bf16),
                pltpu.VMEM((plane, side, pts), bf16),
                pltpu.VMEM((side, side), f32),
                pltpu.VMEM((4, 16, pts), f32),
                pltpu.VMEM((4, 1, pts), f32),
                pltpu.VMEM((4, 4, pts), f32),
                pltpu.VMEM((4, 4, pts), f32),
                pltpu.VMEM((2, pts), f32),
                pltpu.VMEM((plane, 2, pts), f32),
                pltpu.VMEM((4 * side, side), f32),
                pltpu.VMEM((ITERS - 1, 2, side, side), f32),
                pltpu.VMEM((ITERS, 2, side, side), f32),
                pltpu.VMEM((ITERS, 2, side, side), f32),
                pltpu.VMEM((ITERS, 4, 2, side), f32),
                pltpu.VMEM((ITERS, 4, 2, side), f32),
                dma((6,)), dma((6,)),
                dma((3,)), dma((3,)),
                dma((9,)), dma((9,)),
                dma((3,)), dma((3,)), dma((4,)),
                dma((plane,)), dma((plane,)),
                dma((plane,)), dma((plane,)),
                dma((3,)), dma((3,)),
                dma((ITERS, 6)), dma((ITERS, 6)),
            ],
            compiler_params=pltpu.CompilerParams(
                collective_id=0, has_side_effects=True, vmem_limit_bytes=56 * 1024 * 1024
            ),
        )(blocks, count, desc, pos, ids, disp, stiff)
        return moved[None]

    in_specs = (
        P("sec", "ty", "tx", None, None),
        P("sec", "ty", "tx", None, None),
        P("sec", "ty", "tx", None),
        P("sec", "ty", "tx", None),
        P("sec", "ty", "tx"),
        P("sec", None, "ty", "tx"),
        P("sec", "ty", "tx"),
    )
    return jax.shard_map(
        per_device, mesh=mesh, in_specs=in_specs, out_specs=P("sec", None, "ty", "tx"), check_vma=False
    )
```

```python
import functools
import math

import jax
import jax.numpy as jnp
from jax import lax
from jax.experimental import pallas as pl
from jax.experimental.pallas import tpu as pltpu
from jax.sharding import PartitionSpec as P

MESH = pl.DeviceIdType.MESH
BLK = 128
CAPB = 4
CHUNK = 256
ITERS = 4
NEG = -1e30
SPRING_SEC = 0.5
RATE = 0.8
NT = (((1,), (1,)), ((), ()))
NN = (((1,), (0,)), ((), ()))


def remote(src, dst, send, recv, device):
    return pltpu.make_async_remote_copy(
        src_ref=src, dst_ref=dst, send_sem=send, recv_sem=recv, device_id=device, device_id_type=MESH
    )


def block_table(list_ref, count_ref, slots):
    lane = lax.broadcasted_iota(jnp.int32, (8, 128), 1)
    row = lax.broadcasted_iota(jnp.int32, (8, 128), 0)
    within = lane & 7
    wanted = jnp.zeros((8, 128), jnp.int32)
    for entry in range(slots):
        block = jnp.where(count_ref[0, 0, 0] > entry, list_ref[entry], -1)
        wanted = jnp.where(lane == block, 1, wanted)
    rank = jnp.zeros((8, 128), jnp.int32)
    for by in range(1, 8):
        rank = rank + jnp.where(within >= by, pltpu.roll(wanted, by, 1), 0)
    picked = jnp.where((wanted == 1) & (rank == row), within + 1, 0)
    total = picked
    for by in range(1, 8):
        total = total + pltpu.roll(picked, 128 - by, 1)
    return jnp.where(total == 0, 8, total - 1)


def kernel(
    sizes, list_ref, count_ref, desc, pos, ids, disp, stiff, out,
    dispv, stiffv, posv, qbuf, kin0, kin1, kin2, kin3, pin, kwork, vwork, tabv, tabs, idb, onea, onec, mcount,
    acc, mx, sbuf0, sbuf1, tops0, tops1, part, prt, pull, pbuf, scat, ub, wire, lob, upb, edge, halo,
    qs, qr, hs, hr, ks, kr, ts, tr, tl, ids_s, ids_r, ps, pr, cs, cr, us, ur, ls, gossip,
):
    ns, ny, nz, slots = sizes
    plane = ny * nz
    pts, feat = desc.shape
    half = pts // 2
    blocks = pts // BLK
    side = stiff.shape[0]
    s, y, z = lax.axis_index("sec"), lax.axis_index("ty"), lax.axis_index("tx")
    me = y * nz + z
    right, left = {"tx": lax.rem(z + 1, nz)}, {"tx": lax.rem(z + nz - 1, nz)}
    across = {"tx": lax.rem(z + 2, nz)}
    down, up = {"ty": lax.rem(y + 1, ny)}, {"ty": lax.rem(y + ny - 1, ny)}
    after, before = {"sec": lax.rem(s + 1, ns)}, {"sec": lax.rem(s + ns - 1, ns)}

    def peer(by):
        tile = lax.rem(me + by, plane)
        return tile, {"ty": lax.div(tile, nz), "tx": lax.rem(tile, nz)}

    barrier = pltpu.get_barrier_semaphore()

    near = (right, left, down, up, after, before)
    for device in near:
        pl.semaphore_signal(barrier, inc=1, device_id=device, device_id_type=MESH)
    loads = [
        pltpu.make_async_copy(desc, qbuf.at[0], ls.at[0]),
        pltpu.make_async_copy(pos, posv, ls.at[1]),
        pltpu.make_async_copy(ids, idb.at[me], ls.at[2]),
        pltpu.make_async_copy(disp, dispv, ls.at[3]),
        pltpu.make_async_copy(stiff, stiffv, ls.at[4]),
    ]
    for copy in loads:
        copy.start()

    tabv[0] = block_table(list_ref, count_ref, slots)
    acc[...] = jnp.zeros_like(acc)
    mx[...] = jnp.full_like(mx, NEG)
    mcount[...] = jnp.zeros_like(mcount)
    scat[...] = jnp.zeros_like(scat)

    pl.semaphore_wait(barrier, len(near))

    rows = [pl.ds(0, half), pl.ds(half, half)]
    shift = [
        remote(desc.at[rows[0]], kin0.at[rows[0]], hs.at[0], hr.at[0], before),
        remote(desc.at[rows[1]], kin0.at[rows[1]], hs.at[1], hr.at[1], before),
        remote(pos, pin.at[0], hs.at[2], hr.at[2], before),
    ]
    tables = [
        remote(tabv.at[0], tabv.at[1], ts.at[0], tr.at[0], right),
        remote(tabv.at[0], tabv.at[2], ts.at[1], tr.at[1], left),
        remote(tabv.at[0], tabv.at[3], ts.at[2], tr.at[2], across),
    ]
    queries = [
        remote(desc.at[rows[0]], qbuf.at[1, rows[0]], qs.at[0], qr.at[0], right),
        remote(desc.at[rows[1]], qbuf.at[2, rows[1]], qs.at[1], qr.at[1], left),
        remote(desc.at[rows[1]], qbuf.at[1, rows[1]], qs.at[2], qr.at[2], right),
        remote(desc.at[rows[0]], qbuf.at[2, rows[0]], qs.at[3], qr.at[3], left),
        remote(qbuf.at[1, rows[0]], qbuf.at[3, rows[0]], qs.at[4], qr.at[4], right),
        remote(qbuf.at[2, rows[1]], qbuf.at[3, rows[1]], qs.at[5], qr.at[5], left),
    ]
    keys = [
        remote(kin0.at[rows[0]], kin1.at[rows[0]], ks.at[0], kr.at[0], down),
        remote(kin0.at[rows[1]], kin2.at[rows[1]], ks.at[1], kr.at[1], up),
        remote(kin0.at[rows[1]], kin1.at[rows[1]], ks.at[2], kr.at[2], down),
        remote(kin0.at[rows[0]], kin2.at[rows[0]], ks.at[3], kr.at[3], up),
        remote(kin1.at[rows[0]], kin3.at[rows[0]], ks.at[4], kr.at[4], down),
        remote(kin2.at[rows[1]], kin3.at[rows[1]], ks.at[5], kr.at[5], up),
        remote(pin.at[0], pin.at[1], ks.at[6], kr.at[6], down),
        remote(pin.at[0], pin.at[2], ks.at[7], kr.at[7], up),
        remote(pin.at[1], pin.at[3], ks.at[8], kr.at[8], down),
    ]
    partials = [
        remote(part.at[1], prt.at[2], cs.at[0], cr.at[0], left),
        remote(part.at[2], prt.at[1], cs.at[1], cr.at[1], right),
        remote(part.at[3], prt.at[3], cs.at[2], cr.at[2], across),
    ]

    def exchange(turn):
        return [
            remote(edge.at[turn, 0], halo.at[turn, 1], us.at[turn, 0], ur.at[turn, 0], up),
            remote(edge.at[turn, 1], halo.at[turn, 0], us.at[turn, 1], ur.at[turn, 1], down),
            remote(edge.at[turn, 2], halo.at[turn, 3], us.at[turn, 2], ur.at[turn, 2], left),
            remote(edge.at[turn, 3], halo.at[turn, 2], us.at[turn, 3], ur.at[turn, 3], right),
            remote(wire.at[turn, 0], lob.at[turn, 0], us.at[turn, 4], ur.at[turn, 4], after),
            remote(wire.at[turn, 0], upb.at[turn, 0], us.at[turn, 5], ur.at[turn, 5], before),
            remote(wire.at[turn, 1], lob.at[turn, 1], us.at[turn, 6], ur.at[turn, 6], after),
            remote(wire.at[turn, 1], upb.at[turn, 1], us.at[turn, 7], ur.at[turn, 7], before),
        ]

    swaps = [exchange(turn) for turn in range(ITERS)]

    def ids_copy(by):
        _, device = peer(by)
        return remote(ids, idb.at[me], ids_s.at[by], ids_r.at[me], device)

    def ids_from(tile):
        return remote(ids, idb.at[tile], ids_s.at[0], ids_r.at[tile], before)

    def pull_copy(by):
        _, device = peer(by)
        return remote(pull, pbuf.at[me], ps.at[by], pr.at[me], device)

    def pull_from(tile):
        return remote(pull, pbuf.at[tile], ps.at[0], pr.at[tile], before)

    def start_ids(by, carry):
        ids_copy(by).start()
        return carry

    for copy in shift[:2] + tables[:2] + queries[:2] + shift[2:]:
        copy.start()
    for at, pair in enumerate(((right, left), (down, up), (down, up))):
        for device in pair:
            pl.semaphore_signal(gossip.at[at], inc=1, device_id=device, device_id_type=MESH)
        pl.semaphore_wait(gossip.at[at], 2)
    lax.fori_loop(1, plane, start_ids, 0)
    tables[2].start()
    for copy in queries[2:4]:
        copy.start()
    for copy in loads:
        copy.wait()

    def set_key(slot, source):
        kwork[slot] = source[...].reshape(blocks, BLK, feat)
        place = pin[slot].astype(jnp.float32)
        line = lax.broadcasted_iota(jnp.int32, (16, pts), 0)
        value = jnp.where(line == 2, 1.0, 0.0)
        value = jnp.where(line == 1, place[1:2], value)
        value = jnp.where(line == 0, place[0:1], value).astype(jnp.bfloat16)
        for block in range(blocks):
            vwork[slot, block] = value[:, block * BLK : (block + 1) * BLK]

    eye = lax.broadcasted_iota(jnp.int32, (side, side), 0) == lax.broadcasted_iota(jnp.int32, (side, side), 1)

    def set_edges(turn, channel, value):
        edge[turn, 0, channel : channel + 1, :] = value[0:1, :]
        edge[turn, 1, channel : channel + 1, :] = value[side - 1 : side, :]
        for at, column in ((2, value[:, 0:1]), (3, value[:, side - 1 : side])):
            spread = jnp.where(eye, jnp.broadcast_to(column, (side, side)), 0.0)
            edge[turn, at, channel : channel + 1, :] = jnp.sum(spread, axis=0, keepdims=True)

    for channel in range(2):
        set_edges(0, channel, dispv[channel])
        wire[0, channel] = dispv[channel].astype(jnp.bfloat16)

    def one_hots(by, carry):
        tile, _ = peer(by)

        @pl.when(by > 0)
        def _():
            ids_from(tile).wait_recv()

        vertex = idb[tile]
        level = lax.broadcasted_iota(jnp.int32, (side, pts), 0)
        pick_row = level == ((vertex - me * (side * side)) >> 7)
        pick_col = level == (vertex & (side - 1))
        row_hot = jnp.where(pick_row, 1.0, 0.0).astype(jnp.bfloat16)
        col_hot = jnp.where(pick_col, 1.0, 0.0).astype(jnp.bfloat16)
        onea[tile] = row_hot
        onec[tile] = col_hot
        mcount[...] += lax.dot_general(row_hot, col_hot, NT, preferred_element_type=jnp.float32)
        return carry

    factor = 16.0 / feat * math.log2(math.e)

    def found(step):
        q, k = lax.div(step, 4), lax.rem(step, 4)
        key_row = lax.rem(y + jnp.where(k == 1, ny - 1, jnp.where(k == 2, 1, jnp.where(k == 3, 2, 0))), ny)
        lane = (key_row * nz + z) * 8
        codes = [tabs[q, slot, lane] for slot in range(CAPB)]
        return q, k, [code & (blocks - 1) for code in codes], [code < blocks for code in codes]

    chunks = [pl.ds(at * CHUNK, CHUNK) for at in range(pts // CHUNK)]

    def scorer(step, sbuf, tops):
        q, k, at_block, live = found(step)
        key_rows = jnp.concatenate([kwork[k, block] for block in at_block], axis=0)

        def score(cols):
            raw = lax.dot_general(key_rows, qbuf[q, cols, :], NT, preferred_element_type=jnp.float32)
            sbuf[:, cols] = raw
            for i in range(CAPB):
                top = jnp.max(raw[i * BLK : (i + 1) * BLK], axis=0, keepdims=True)
                tops[i, :, cols] = jnp.where(live[i], top, NEG)

        return score

    def weigher(step, sbuf, tops):
        q, k, at_block, live = found(step)
        values = jnp.concatenate([vwork[k, block] for block in at_block], axis=1)

        def weigh(cols):
            old = mx[q, :, cols]
            new = functools.reduce(jnp.maximum, [tops[i, :, cols] for i in range(CAPB)], old)
            weights = []
            for i in range(CAPB):
                base = jnp.where(live[i], new, -NEG)
                raw = sbuf[i * BLK : (i + 1) * BLK, cols]
                weights.append(jnp.exp2((raw - base) * factor).astype(jnp.bfloat16))
            added = lax.dot_general(
                values, jnp.concatenate(weights, axis=0), NN, preferred_element_type=jnp.float32
            )
            acc[q, :, cols] = acc[q, :, cols] * jnp.exp2((old - new) * factor) + added
            mx[q, :, cols] = new

        return weigh

    def match(step, carry):
        @pl.when(step == 0)
        def _():
            queries[0].wait_recv()
            queries[4].start()
            queries[1].wait_recv()
            queries[5].start()
            keys[0].wait_recv()
            keys[4].start()
            keys[1].wait_recv()
            keys[5].start()
            keys[6].wait_recv()
            keys[8].start()
            lax.fori_loop(0, plane, one_hots, 0)
            keys[2].wait_recv()
            set_key(1, kin1)

        @pl.when(step == 1)
        def _():
            keys[3].wait_recv()
            keys[7].wait_recv()
            set_key(2, kin2)

        @pl.when(step == 2)
        def _():
            keys[4].wait_recv()
            keys[5].wait_recv()
            keys[8].wait_recv()
            set_key(3, kin3)

        for slot in range(1, 4):

            @pl.when(step == 4 * slot - 1)
            def _():
                for copy in ((), (2,), (3,), (4, 5))[slot]:
                    queries[copy].wait_recv()
                tables[slot - 1].wait_recv()
                local = pltpu.make_async_copy(tabv.at[slot], tabs.at[slot], tl.at[slot])
                local.start()
                local.wait()

        @pl.when(step == 10)
        def _():
            for copy in swaps[0]:
                copy.start()

        following = lax.rem(step + 1, 16)
        for parity, first, second in ((0, (sbuf0, tops0), (sbuf1, tops1)), (1, (sbuf1, tops1), (sbuf0, tops0))):

            @pl.when(lax.rem(step, 2) == parity)
            def _():
                score, weigh = scorer(following, *second), weigher(step, *first)
                for cols in chunks:
                    weigh(cols)
                    score(cols)

        q, k = lax.div(step, 4), lax.rem(step, 4)

        @pl.when(k == 3)
        def _():
            part[q, 0:3, :] = acc[q, 0:3, :]
            part[q, 3:4, :] = mx[q]

        for slot in range(1, 4):

            @pl.when(step == 4 * slot + 3)
            def _():
                partials[slot - 1].start()

        return carry

    local = pltpu.make_async_copy(tabv.at[0], tabs.at[0], tl.at[0])
    local.start()
    local.wait()
    shift[0].wait_recv()
    keys[0].start()
    shift[1].wait_recv()
    keys[1].start()
    keys[2].start()
    keys[3].start()
    shift[2].wait_recv()
    keys[6].start()
    keys[7].start()
    set_key(0, kin0)
    score = scorer(jnp.int32(0), sbuf0, tops0)
    for cols in chunks:
        score(cols)
    lax.fori_loop(0, 16, match, 0)

    has_next = s < ns - 1
    for copy in partials:
        copy.wait_recv()
    pieces = [part[0]] + [prt[slot] for slot in range(1, 4)]
    top = functools.reduce(jnp.maximum, [piece[3:4] for piece in pieces])
    scaled = [piece[0:3] * jnp.exp2((piece[3:4] - top) * factor) for piece in pieces]
    total = functools.reduce(jnp.add, scaled)
    mine = posv[...].astype(jnp.float32)
    pull[...] = jnp.where(has_next, total[0:2] / total[2:3] - mine, 0.0)

    def start_pull(by, carry):
        pull_copy(by).start()
        return carry

    lax.fori_loop(1, plane, start_pull, 0)
    pbuf[pl.ds(me, 1)] = pull[...][None]

    order = [(0, 0), (1, 0), (3, 0), (2, 0), (0, 1), (0, 3), (1, 1), (3, 1), (1, 3), (3, 3)]
    order += [(2, 1), (2, 3), (0, 2), (1, 2), (3, 2), (2, 2)]
    wrap = lambda value: value - (1 << 32) if value >= 1 << 31 else value
    code_y = wrap(sum(dy << (2 * at) for at, (dy, _) in enumerate(order)))
    code_z = wrap(sum(dz << (2 * at) for at, (_, dz) in enumerate(order)))

    def gather_pull(turn, carry):
        ahead_y = (jnp.int32(code_y) >> (2 * turn)) & 3
        ahead_z = (jnp.int32(code_z) >> (2 * turn)) & 3
        tile = lax.rem(y + ahead_y, ny) * nz + lax.rem(z + ahead_z, nz)

        @pl.when(turn > 0)
        def _():
            pull_from(tile).wait_recv()

        row_hot = onea[tile].reshape(side // 16, 16, pts)
        pieces = []
        for channel in range(2):
            value = jnp.broadcast_to(pbuf[tile, channel : channel + 1, :], (16, pts))
            high = value.astype(jnp.bfloat16)
            low = (value - high.astype(jnp.float32)).astype(jnp.bfloat16)
            for piece in (high, low):
                pieces.append((row_hot * piece[None]).reshape(side, pts))
        stacked = jnp.concatenate(pieces, axis=0)
        scat[...] += lax.dot_general(stacked, onec[tile], NT, preferred_element_type=jnp.float32)
        return carry

    lax.fori_loop(0, plane, gather_pull, 0)

    flag = lambda test: jnp.where(test, 1.0, 0.0)
    next_flag, last_flag = flag(s < ns - 1), flag(s > 0)
    linked = next_flag + last_flag
    matched = mcount[...] * next_flag
    gains = stiffv[...]
    inverse = RATE / (4.0 * gains + SPRING_SEC * linked + matched)
    pulled = [scat[0:side] + scat[side : 2 * side], scat[2 * side : 3 * side] + scat[3 * side :]]
    row_at = lax.broadcasted_iota(jnp.int32, (side, side), 0)
    col_at = lax.broadcasted_iota(jnp.int32, (side, side), 1)
    flags = [flag(y > 0), flag(y < ny - 1), flag(z > 0), flag(z < nz - 1)]

    for turn in range(ITERS):
        for copy in swaps[turn]:
            copy.wait_recv()
        for channel in range(2):
            value = dispv[channel] if turn == 0 else ub[turn - 1, channel]
            lines = [halo[turn, at, channel : channel + 1, :] * flags[at] for at in range(4)]
            cols = [
                jnp.sum(jnp.where(eye, jnp.broadcast_to(line, (side, side)), 0.0), axis=1, keepdims=True)
                for line in lines[2:]
            ]
            around = jnp.where(row_at == 0, lines[0], pltpu.roll(value, 1, 0))
            around += jnp.where(row_at == side - 1, lines[1], pltpu.roll(value, side - 1, 0))
            around += jnp.where(col_at == 0, cols[0], pltpu.roll(value, 1, 1))
            around += jnp.where(col_at == side - 1, cols[1], pltpu.roll(value, side - 1, 1))
            force = gains * (around - 4.0 * value) + pulled[channel] - matched * value
            force += SPRING_SEC * (
                lob[turn, channel].astype(jnp.float32) * last_flag
                + upb[turn, channel].astype(jnp.float32) * next_flag
                - linked * value
            )
            moved = value + force * inverse
            if turn == ITERS - 1:
                out[channel] = moved
            else:
                wire[turn + 1, channel] = moved.astype(jnp.bfloat16)
                for copy in swaps[turn + 1][4 + 2 * channel : 6 + 2 * channel]:
                    copy.start()
                ub[turn, channel] = moved
                set_edges(turn + 1, channel, moved)
        if turn < ITERS - 1:
            for copy in swaps[turn + 1][:4]:
                copy.start()

    for copy in shift + tables + queries + keys + partials + [c for swap in swaps for c in swap]:
        copy.wait_send()

    def finish(by, carry):
        ids_copy(by).wait_send()
        pull_copy(by).wait_send()
        return carry

    lax.fori_loop(1, plane, finish, 0)


def solution(mesh):
    ns, ny, nz = mesh.shape["sec"], mesh.shape["ty"], mesh.shape["tx"]

    def per_device(desc, pos, ids, blocks, count, disp, stiff):
        desc, pos, ids = desc[0, 0, 0], pos[0, 0, 0], ids[0, 0]
        blocks = blocks[0, 0, 0]
        disp, stiff = disp[0], stiff[0]
        pts, feat = desc.shape
        side = stiff.shape[0]
        plane = ny * nz
        bf16, f32, i32 = jnp.bfloat16, jnp.float32, jnp.int32
        tile = pltpu.VMEM((pts, feat), bf16)
        dma = pltpu.SemaphoreType.DMA
        smem = pl.BlockSpec(memory_space=pltpu.SMEM)
        vmem = pl.BlockSpec(memory_space=pltpu.VMEM)
        moved = pl.pallas_call(
            functools.partial(kernel, (ns, ny, nz, blocks.shape[0])),
            out_shape=jax.ShapeDtypeStruct(disp.shape, f32),
            in_specs=[smem, smem] + [pl.BlockSpec(memory_space=pl.ANY)] * 5,
            out_specs=vmem,
            scratch_shapes=[
                pltpu.VMEM((2, side, side), f32),
                pltpu.VMEM((side, side), f32),
                pltpu.VMEM((2, pts), bf16),
                pltpu.VMEM((4, pts, feat), bf16),
                tile, tile, tile, tile,
                pltpu.VMEM((4, 2, pts), bf16),
                pltpu.VMEM((4, pts // BLK, BLK, feat), bf16),
                pltpu.VMEM((4, pts // BLK, 16, BLK), bf16),
                pltpu.VMEM((4, 8, 128), i32),
                pltpu.SMEM((4, 8, 128), i32),
                pltpu.VMEM((plane, 1, pts), i32),
                pltpu.VMEM((plane, side, pts), bf16),
                pltpu.VMEM((plane, side, pts), bf16),
                pltpu.VMEM((side, side), f32),
                pltpu.VMEM((4, 16, pts), f32),
                pltpu.VMEM((4, 1, pts), f32),
                pltpu.VMEM((CAPB * BLK, pts), f32),
                pltpu.VMEM((CAPB * BLK, pts), f32),
                pltpu.VMEM((CAPB, 1, pts), f32),
                pltpu.VMEM((CAPB, 1, pts), f32),
                pltpu.VMEM((4, 4, pts), f32),
                pltpu.VMEM((4, 4, pts), f32),
                pltpu.VMEM((2, pts), f32),
                pltpu.VMEM((plane, 2, pts), f32),
                pltpu.VMEM((4 * side, side), f32),
                pltpu.VMEM((ITERS - 1, 2, side, side), f32),
                pltpu.VMEM((ITERS, 2, side, side), bf16),
                pltpu.VMEM((ITERS, 2, side, side), bf16),
                pltpu.VMEM((ITERS, 2, side, side), bf16),
                pltpu.VMEM((ITERS, 4, 2, side), f32),
                pltpu.VMEM((ITERS, 4, 2, side), f32),
                dma((6,)), dma((6,)),
                dma((3,)), dma((3,)),
                dma((9,)), dma((9,)),
                dma((3,)), dma((3,)), dma((4,)),
                dma((plane,)), dma((plane,)),
                dma((plane,)), dma((plane,)),
                dma((3,)), dma((3,)),
                dma((ITERS, 8)), dma((ITERS, 8)),
                dma((5,)), pltpu.SemaphoreType.REGULAR((3,)),
            ],
            compiler_params=pltpu.CompilerParams(
                collective_id=0, has_side_effects=True, vmem_limit_bytes=56 * 1024 * 1024
            ),
        )(blocks, count, desc, pos, ids, disp, stiff)
        return moved[None]

    in_specs = (
        P("sec", "ty", "tx", None, None),
        P("sec", "ty", "tx", None, None),
        P("sec", "ty", "tx", None),
        P("sec", "ty", "tx", None),
        P("sec", "ty", "tx"),
        P("sec", None, "ty", "tx"),
        P("sec", "ty", "tx"),
    )
    return jax.shard_map(
        per_device, mesh=mesh, in_specs=in_specs, out_specs=P("sec", None, "ty", "tx"), check_vma=False
    )
```

```python
import functools
import math

import jax
import jax.numpy as jnp
from jax import lax
from jax.experimental import pallas as pl
from jax.experimental.pallas import tpu as pltpu
from jax.sharding import PartitionSpec as P

MESH = pl.DeviceIdType.MESH
BLK = 128
CAPB = 4
CHUNK = 256
ITERS = 4
NEG = -1e30
SPRING_SEC = 0.5
RATE = 0.8
NT = (((1,), (1,)), ((), ()))
NN = (((1,), (0,)), ((), ()))


def remote(src, dst, send, recv, device):
    return pltpu.make_async_remote_copy(
        src_ref=src, dst_ref=dst, send_sem=send, recv_sem=recv, device_id=device, device_id_type=MESH
    )


def block_table(list_ref, count_ref, slots):
    lane = lax.broadcasted_iota(jnp.int32, (8, 128), 1)
    row = lax.broadcasted_iota(jnp.int32, (8, 128), 0)
    within = lane & 7
    wanted = jnp.zeros((8, 128), jnp.int32)
    for entry in range(slots):
        block = jnp.where(count_ref[0, 0, 0] > entry, list_ref[entry], -1)
        wanted = jnp.where(lane == block, 1, wanted)
    rank = jnp.zeros((8, 128), jnp.int32)
    for by in range(1, 8):
        rank = rank + jnp.where(within >= by, pltpu.roll(wanted, by, 1), 0)
    picked = jnp.where((wanted == 1) & (rank == row), within + 1, 0)
    total = picked
    for by in range(1, 8):
        total = total + pltpu.roll(picked, 128 - by, 1)
    return jnp.where(total == 0, 8, total - 1)


def kernel(
    sizes, list_ref, count_ref, desc, pos, ids, disp, stiff, out,
    dispv, stiffv, posv, qbuf, kin0, kin1, kin2, kin3, pin, kwork, vwork, tabv, tabs, idb, onea, onec, mcount,
    acc, mx, sbuf0, sbuf1, tops0, tops1, part, prt, pull, pbuf, scat, ub, wire, lob, upb, edge, halo,
    qs, qr, hs, hr, ks, kr, ts, tr, tl, ids_s, ids_r, ps, pr, cs, cr, us, ur, ls,
):
    ns, ny, nz, slots = sizes
    plane = ny * nz
    pts, feat = desc.shape
    half = pts // 2
    blocks = pts // BLK
    side = stiff.shape[0]
    s, y, z = lax.axis_index("sec"), lax.axis_index("ty"), lax.axis_index("tx")
    me = y * nz + z
    right, left = {"tx": lax.rem(z + 1, nz)}, {"tx": lax.rem(z + nz - 1, nz)}
    across = {"tx": lax.rem(z + 2, nz)}
    down, up = {"ty": lax.rem(y + 1, ny)}, {"ty": lax.rem(y + ny - 1, ny)}
    after, before = {"sec": lax.rem(s + 1, ns)}, {"sec": lax.rem(s + ns - 1, ns)}

    def peer(by):
        tile = lax.rem(me + by, plane)
        return tile, {"ty": lax.div(tile, nz), "tx": lax.rem(tile, nz)}

    barrier = pltpu.get_barrier_semaphore()

    near = (right, left, down, up, after, before)
    for device in near:
        pl.semaphore_signal(barrier, inc=1, device_id=device, device_id_type=MESH)
    loads = [
        pltpu.make_async_copy(desc, qbuf.at[0], ls.at[0]),
        pltpu.make_async_copy(pos, posv, ls.at[1]),
        pltpu.make_async_copy(ids, idb.at[me], ls.at[2]),
        pltpu.make_async_copy(disp, dispv, ls.at[3]),
        pltpu.make_async_copy(stiff, stiffv, ls.at[4]),
    ]
    for copy in loads:
        copy.start()

    tabv[0] = block_table(list_ref, count_ref, slots)
    acc[...] = jnp.zeros_like(acc)
    mx[...] = jnp.full_like(mx, NEG)
    mcount[...] = jnp.zeros_like(mcount)
    scat[...] = jnp.zeros_like(scat)

    pl.semaphore_wait(barrier, len(near))

    rows = [pl.ds(0, half), pl.ds(half, half)]
    shift = [
        remote(desc.at[rows[0]], kin0.at[rows[0]], hs.at[0], hr.at[0], before),
        remote(desc.at[rows[1]], kin0.at[rows[1]], hs.at[1], hr.at[1], before),
        remote(pos, pin.at[0], hs.at[2], hr.at[2], before),
    ]
    tables = [
        remote(tabv.at[0], tabv.at[1], ts.at[0], tr.at[0], right),
        remote(tabv.at[0], tabv.at[2], ts.at[1], tr.at[1], left),
        remote(tabv.at[1], tabv.at[3], ts.at[2], tr.at[2], right),
    ]
    piece = [pl.ds(at * CHUNK, CHUNK) for at in range(pts // CHUNK)]
    to_right = [remote(desc.at[piece[at]], qbuf.at[1, piece[at]], qs.at[at], qr.at[at], right) for at in range(4)]
    to_left = [
        remote(desc.at[piece[at]], qbuf.at[2, piece[at]], qs.at[4 + at], qr.at[4 + at], left)
        for at in (2, 3, 0, 1)
    ]
    on_right = [
        remote(qbuf.at[1, piece[at]], qbuf.at[3, piece[at]], qs.at[8 + at], qr.at[8 + at], right) for at in (0, 1)
    ]
    on_left = [
        remote(qbuf.at[2, piece[at]], qbuf.at[3, piece[at]], qs.at[8 + at], qr.at[8 + at], left) for at in (2, 3)
    ]
    queries = to_right + to_left + on_right + on_left
    lefts = y * nz + lax.rem(z + nz - 1, nz)
    row, row_up = pl.ds(y * nz, nz), pl.ds(lax.rem(y + ny - 1, ny) * nz, nz)
    names = [
        remote(ids, idb.at[me], ids_s.at[0], ids_r.at[0], right),
        remote(ids, idb.at[me], ids_s.at[1], ids_r.at[1], left),
        remote(idb.at[lefts], idb.at[lefts], ids_s.at[2], ids_r.at[2], right),
        remote(idb.at[row], idb.at[row], ids_s.at[3], ids_r.at[3], down),
        remote(idb.at[row], idb.at[row], ids_s.at[4], ids_r.at[4], up),
        remote(idb.at[row_up], idb.at[row_up], ids_s.at[5], ids_r.at[5], down),
    ]
    keys = [
        remote(kin0.at[rows[0]], kin1.at[rows[0]], ks.at[0], kr.at[0], down),
        remote(kin0.at[rows[1]], kin2.at[rows[1]], ks.at[1], kr.at[1], up),
        remote(kin0.at[rows[1]], kin1.at[rows[1]], ks.at[2], kr.at[2], down),
        remote(kin0.at[rows[0]], kin2.at[rows[0]], ks.at[3], kr.at[3], up),
        remote(kin1.at[rows[0]], kin3.at[rows[0]], ks.at[4], kr.at[4], down),
        remote(kin2.at[rows[1]], kin3.at[rows[1]], ks.at[5], kr.at[5], up),
        remote(pin.at[0], pin.at[1], ks.at[6], kr.at[6], down),
        remote(pin.at[0], pin.at[2], ks.at[7], kr.at[7], up),
        remote(pin.at[1], pin.at[3], ks.at[8], kr.at[8], down),
    ]
    partials = [
        remote(part.at[1], prt.at[2], cs.at[0], cr.at[0], left),
        remote(part.at[2], prt.at[1], cs.at[1], cr.at[1], right),
        remote(part.at[3], prt.at[3], cs.at[2], cr.at[2], across),
    ]

    def exchange(turn):
        return [
            remote(edge.at[turn, 0], halo.at[turn, 1], us.at[turn, 0], ur.at[turn, 0], up),
            remote(edge.at[turn, 1], halo.at[turn, 0], us.at[turn, 1], ur.at[turn, 1], down),
            remote(edge.at[turn, 2], halo.at[turn, 3], us.at[turn, 2], ur.at[turn, 2], left),
            remote(edge.at[turn, 3], halo.at[turn, 2], us.at[turn, 3], ur.at[turn, 3], right),
            remote(wire.at[turn, 0], lob.at[turn, 0], us.at[turn, 4], ur.at[turn, 4], after),
            remote(wire.at[turn, 0], upb.at[turn, 0], us.at[turn, 5], ur.at[turn, 5], before),
            remote(wire.at[turn, 1], lob.at[turn, 1], us.at[turn, 6], ur.at[turn, 6], after),
            remote(wire.at[turn, 1], upb.at[turn, 1], us.at[turn, 7], ur.at[turn, 7], before),
        ]

    swaps = [exchange(turn) for turn in range(ITERS)]

    def pull_copy(by):
        _, device = peer(by)
        return remote(pull, pbuf.at[me], ps.at[by], pr.at[me], device)

    def pull_from(tile):
        return remote(pull, pbuf.at[tile], ps.at[0], pr.at[tile], before)

    for copy in shift + tables[:2] + names[:2]:
        copy.start()
    for at in range(3):
        to_right[at].start()
        to_left[at].start()
    for copy in loads:
        copy.wait()

    def set_key(slot, source):
        kwork[slot] = source[...].reshape(blocks, BLK, feat)
        place = pin[slot].astype(jnp.float32)
        line = lax.broadcasted_iota(jnp.int32, (16, pts), 0)
        value = jnp.where(line == 2, 1.0, 0.0)
        value = jnp.where(line == 1, place[1:2], value)
        value = jnp.where(line == 0, place[0:1], value).astype(jnp.bfloat16)
        for block in range(blocks):
            vwork[slot, block] = value[:, block * BLK : (block + 1) * BLK]

    eye = lax.broadcasted_iota(jnp.int32, (side, side), 0) == lax.broadcasted_iota(jnp.int32, (side, side), 1)

    def set_edges(turn, channel, value):
        edge[turn, 0, channel : channel + 1, :] = value[0:1, :]
        edge[turn, 1, channel : channel + 1, :] = value[side - 1 : side, :]
        for at, column in ((2, value[:, 0:1]), (3, value[:, side - 1 : side])):
            spread = jnp.where(eye, jnp.broadcast_to(column, (side, side)), 0.0)
            edge[turn, at, channel : channel + 1, :] = jnp.sum(spread, axis=0, keepdims=True)

    for channel in range(2):
        set_edges(0, channel, dispv[channel])
        wire[0, channel] = dispv[channel].astype(jnp.bfloat16)

    order = [(0, 0), (1, 0), (3, 0), (2, 0), (0, 1), (0, 3), (1, 1), (3, 1), (1, 3), (3, 3)]
    order += [(2, 1), (2, 3), (0, 2), (1, 2), (3, 2), (2, 2)]
    wrap = lambda value: value - (1 << 32) if value >= 1 << 31 else value
    code_y = wrap(sum(dy << (2 * at) for at, (dy, _) in enumerate(order)))
    code_z = wrap(sum(dz << (2 * at) for at, (_, dz) in enumerate(order)))

    def nearest(turn):
        ahead_y = (jnp.int32(code_y) >> (2 * turn)) & 3
        ahead_z = (jnp.int32(code_z) >> (2 * turn)) & 3
        return lax.rem(y + ahead_y, ny) * nz + lax.rem(z + ahead_z, nz)

    def one_hots(turn, carry):
        tile = nearest(turn)

        vertex = idb[tile]
        level = lax.broadcasted_iota(jnp.int32, (side, pts), 0)
        pick_row = level == ((vertex - me * (side * side)) >> 7)
        pick_col = level == (vertex & (side - 1))
        row_hot = jnp.where(pick_row, 1.0, 0.0).astype(jnp.bfloat16)
        col_hot = jnp.where(pick_col, 1.0, 0.0).astype(jnp.bfloat16)
        onea[tile] = row_hot
        onec[tile] = col_hot
        mcount[...] += lax.dot_general(row_hot, col_hot, NT, preferred_element_type=jnp.float32)
        return carry

    factor = 16.0 / feat * math.log2(math.e)

    def packed(values, at):
        return (jnp.int32(sum(value << (2 * i) for i, value in enumerate(values))) >> (2 * at)) & 3

    def unit(step):
        early = step < 16
        quarter, rest = lax.div(step, 4), lax.rem(step, 4)
        pair, k = jnp.where(early, rest, quarter), jnp.where(early, quarter, rest)
        parts = []
        for slots, places in (
            ((0, 0, 1, 1, 1, 3, 3, 1), (0, 2, 0, 1, 2, 0, 1, 3)),
            ((0, 0, 2, 2, 2, 3, 3, 2), (1, 3, 2, 3, 0, 2, 3, 1)),
        ):
            q = packed(slots, pair)
            start = pl.multiple_of(packed(places, pair) * CHUNK, CHUNK)
            key_row = lax.rem(y + packed((0, ny - 1, 1, 2), k), ny)
            lane = (key_row * nz + z) * 8
            codes = [tabs[q, slot, lane] for slot in range(CAPB)]
            parts.append(
                (q, k, pl.ds(start, CHUNK), [code & (blocks - 1) for code in codes], [code < blocks for code in codes])
            )
        return parts

    def score(part_at, sbuf, tops, at):
        q, k, cols, at_block, live = part_at
        key_rows = jnp.concatenate([kwork[k, block] for block in at_block], axis=0)
        raw = lax.dot_general(key_rows, qbuf[q, cols, :], NT, preferred_element_type=jnp.float32)
        sbuf[at] = raw
        for i in range(CAPB):
            top = jnp.max(raw[i * BLK : (i + 1) * BLK], axis=0, keepdims=True)
            tops[at, i] = jnp.where(live[i], top, NEG)

    def weigh(part_at, sbuf, tops, at):
        q, k, cols, at_block, live = part_at
        values = jnp.concatenate([vwork[k, block] for block in at_block], axis=1)
        old = mx[q, :, cols]
        new = functools.reduce(jnp.maximum, [tops[at, i] for i in range(CAPB)], old)
        weights = []
        for i in range(CAPB):
            base = jnp.where(live[i], new, -NEG)
            raw = sbuf[at, i * BLK : (i + 1) * BLK, :]
            weights.append(jnp.exp2((raw - base) * factor).astype(jnp.bfloat16))
        added = lax.dot_general(values, jnp.concatenate(weights, axis=0), NN, preferred_element_type=jnp.float32)
        acc[q, :, cols] = acc[q, :, cols] * jnp.exp2((old - new) * factor) + added
        mx[q, :, cols] = new

    def load_table(slot):
        local = pltpu.make_async_copy(tabv.at[slot], tabs.at[slot], tl.at[slot])
        local.start()
        local.wait()

    def settle(slot):
        part[slot, 0:3, :] = acc[slot, 0:3, :]
        part[slot, 3:4, :] = mx[slot]

    def match(step, carry):
        @pl.when(step == 1)
        def _():
            keys[0].wait_recv()
            keys[4].start()
            keys[1].wait_recv()
            keys[5].start()
            keys[6].wait_recv()
            keys[8].start()
            to_right[0].wait_recv()
            on_right[0].start()
            to_left[0].wait_recv()
            on_left[0].start()
            for slot in (1, 2):
                tables[slot - 1].wait_recv()
                load_table(slot)
            tables[2].start()
            names[0].wait_recv()
            names[2].start()

        @pl.when(step == 2)
        def _():
            to_right[1].wait_recv()
            on_right[1].start()
            to_left[1].wait_recv()
            on_left[1].start()
            to_right[3].start()
            to_left[3].start()

        @pl.when(step == 3)
        def _():
            keys[2].wait_recv()
            set_key(1, kin1)

        @pl.when(step == 7)
        def _():
            keys[3].wait_recv()
            keys[7].wait_recv()
            set_key(2, kin2)

        @pl.when(step == 11)
        def _():
            keys[4].wait_recv()
            keys[5].wait_recv()
            keys[8].wait_recv()
            set_key(3, kin3)

        @pl.when(step == 15)
        def _():
            to_right[2].wait_recv()
            to_left[2].wait_recv()
            names[1].wait_recv()
            names[2].wait_recv()
            names[3].start()
            names[4].start()

        @pl.when(step == 19)
        def _():
            on_right[0].wait_recv()
            on_left[0].wait_recv()
            tables[2].wait_recv()
            load_table(3)

        @pl.when(step == 23)
        def _():
            on_right[1].wait_recv()
            on_left[1].wait_recv()
            names[3].wait_recv()
            names[5].start()
            for copy in swaps[0]:
                copy.start()

        @pl.when(step == 27)
        def _():
            to_right[3].wait_recv()
            to_left[3].wait_recv()

        for parity, first, second in ((0, (sbuf0, tops0), (sbuf1, tops1)), (1, (sbuf1, tops1), (sbuf0, tops0))):

            @pl.when(lax.rem(step, 2) == parity)
            def _():
                ahead, here = unit(lax.rem(step + 1, 32)), unit(step)
                for at in range(2):
                    score(ahead[at], *second, at)
                for at in range(2):
                    weigh(here[at], *first, at)

        @pl.when(step == 27)
        def _():
            settle(3)
            partials[2].start()

        return carry

    local = pltpu.make_async_copy(tabv.at[0], tabs.at[0], tl.at[0])
    local.start()
    local.wait()
    shift[0].wait_recv()
    keys[0].start()
    shift[1].wait_recv()
    keys[1].start()
    keys[2].start()
    keys[3].start()
    shift[2].wait_recv()
    keys[6].start()
    keys[7].start()
    set_key(0, kin0)
    for at, part_at in enumerate(unit(jnp.int32(0))):
        score(part_at, sbuf0, tops0, at)
    lax.fori_loop(0, 32, match, 0)
    for slot in (1, 2):
        settle(slot)
        partials[slot - 1].start()
    settle(0)
    names[4].wait_recv()
    names[5].wait_recv()
    lax.fori_loop(0, plane // 2, one_hots, 0)

    has_next = s < ns - 1
    for copy in partials:
        copy.wait_recv()
    pieces = [part[0]] + [prt[slot] for slot in range(1, 4)]
    top = functools.reduce(jnp.maximum, [piece[3:4] for piece in pieces])
    scaled = [piece[0:3] * jnp.exp2((piece[3:4] - top) * factor) for piece in pieces]
    total = functools.reduce(jnp.add, scaled)
    mine = posv[...].astype(jnp.float32)
    pull[...] = jnp.where(has_next, total[0:2] / total[2:3] - mine, 0.0)

    def start_pull(by, carry):
        pull_copy(by).start()
        return carry

    lax.fori_loop(1, plane, start_pull, 0)
    pbuf[pl.ds(me, 1)] = pull[...][None]
    lax.fori_loop(plane // 2, plane, one_hots, 0)

    def gather_pull(turn, carry):
        tile = nearest(turn)

        @pl.when(turn > 0)
        def _():
            pull_from(tile).wait_recv()

        row_hot = onea[tile].reshape(side // 16, 16, pts)
        pieces = []
        for channel in range(2):
            value = jnp.broadcast_to(pbuf[tile, channel : channel + 1, :], (16, pts))
            high = value.astype(jnp.bfloat16)
            low = (value - high.astype(jnp.float32)).astype(jnp.bfloat16)
            for piece in (high, low):
                pieces.append((row_hot * piece[None]).reshape(side, pts))
        stacked = jnp.concatenate(pieces, axis=0)
        scat[...] += lax.dot_general(stacked, onec[tile], NT, preferred_element_type=jnp.float32)
        return carry

    lax.fori_loop(0, plane, gather_pull, 0)

    flag = lambda test: jnp.where(test, 1.0, 0.0)
    next_flag, last_flag = flag(s < ns - 1), flag(s > 0)
    linked = next_flag + last_flag
    matched = mcount[...] * next_flag
    gains = stiffv[...]
    inverse = RATE / (4.0 * gains + SPRING_SEC * linked + matched)
    pulled = [scat[0:side] + scat[side : 2 * side], scat[2 * side : 3 * side] + scat[3 * side :]]
    row_at = lax.broadcasted_iota(jnp.int32, (side, side), 0)
    col_at = lax.broadcasted_iota(jnp.int32, (side, side), 1)
    flags = [flag(y > 0), flag(y < ny - 1), flag(z > 0), flag(z < nz - 1)]

    for turn in range(ITERS):
        for copy in swaps[turn]:
            copy.wait_recv()
        for channel in range(2):
            value = dispv[channel] if turn == 0 else ub[turn - 1, channel]
            lines = [halo[turn, at, channel : channel + 1, :] * flags[at] for at in range(4)]
            cols = [
                jnp.sum(jnp.where(eye, jnp.broadcast_to(line, (side, side)), 0.0), axis=1, keepdims=True)
                for line in lines[2:]
            ]
            around = jnp.where(row_at == 0, lines[0], pltpu.roll(value, 1, 0))
            around += jnp.where(row_at == side - 1, lines[1], pltpu.roll(value, side - 1, 0))
            around += jnp.where(col_at == 0, cols[0], pltpu.roll(value, 1, 1))
            around += jnp.where(col_at == side - 1, cols[1], pltpu.roll(value, side - 1, 1))
            force = gains * (around - 4.0 * value) + pulled[channel] - matched * value
            force += SPRING_SEC * (
                lob[turn, channel].astype(jnp.float32) * last_flag
                + upb[turn, channel].astype(jnp.float32) * next_flag
                - linked * value
            )
            moved = value + force * inverse
            if turn == ITERS - 1:
                out[channel] = moved
            else:
                wire[turn + 1, channel] = moved.astype(jnp.bfloat16)
                for copy in swaps[turn + 1][4 + 2 * channel : 6 + 2 * channel]:
                    copy.start()
                ub[turn, channel] = moved
                set_edges(turn + 1, channel, moved)
        if turn < ITERS - 1:
            for copy in swaps[turn + 1][:4]:
                copy.start()

    for copy in shift + tables + names + queries + keys + partials + [c for swap in swaps for c in swap]:
        copy.wait_send()

    def finish(by, carry):
        pull_copy(by).wait_send()
        return carry

    lax.fori_loop(1, plane, finish, 0)


def solution(mesh):
    ns, ny, nz = mesh.shape["sec"], mesh.shape["ty"], mesh.shape["tx"]

    def per_device(desc, pos, ids, blocks, count, disp, stiff):
        desc, pos, ids = desc[0, 0, 0], pos[0, 0, 0], ids[0, 0]
        blocks = blocks[0, 0, 0]
        disp, stiff = disp[0], stiff[0]
        pts, feat = desc.shape
        side = stiff.shape[0]
        plane = ny * nz
        bf16, f32, i32 = jnp.bfloat16, jnp.float32, jnp.int32
        tile = pltpu.VMEM((pts, feat), bf16)
        dma = pltpu.SemaphoreType.DMA
        smem = pl.BlockSpec(memory_space=pltpu.SMEM)
        vmem = pl.BlockSpec(memory_space=pltpu.VMEM)
        moved = pl.pallas_call(
            functools.partial(kernel, (ns, ny, nz, blocks.shape[0])),
            out_shape=jax.ShapeDtypeStruct(disp.shape, f32),
            in_specs=[smem, smem] + [pl.BlockSpec(memory_space=pl.ANY)] * 5,
            out_specs=vmem,
            scratch_shapes=[
                pltpu.VMEM((2, side, side), f32),
                pltpu.VMEM((side, side), f32),
                pltpu.VMEM((2, pts), bf16),
                pltpu.VMEM((4, pts, feat), bf16),
                tile, tile, tile, tile,
                pltpu.VMEM((4, 2, pts), bf16),
                pltpu.VMEM((4, pts // BLK, BLK, feat), bf16),
                pltpu.VMEM((4, pts // BLK, 16, BLK), bf16),
                pltpu.VMEM((4, 8, 128), i32),
                pltpu.SMEM((4, 8, 128), i32),
                pltpu.VMEM((plane, 1, pts), i32),
                pltpu.VMEM((plane, side, pts), bf16),
                pltpu.VMEM((plane, side, pts), bf16),
                pltpu.VMEM((side, side), f32),
                pltpu.VMEM((4, 16, pts), f32),
                pltpu.VMEM((4, 1, pts), f32),
                pltpu.VMEM((2, CAPB * BLK, CHUNK), f32),
                pltpu.VMEM((2, CAPB * BLK, CHUNK), f32),
                pltpu.VMEM((2, CAPB, 1, CHUNK), f32),
                pltpu.VMEM((2, CAPB, 1, CHUNK), f32),
                pltpu.VMEM((4, 4, pts), f32),
                pltpu.VMEM((4, 4, pts), f32),
                pltpu.VMEM((2, pts), f32),
                pltpu.VMEM((plane, 2, pts), f32),
                pltpu.VMEM((4 * side, side), f32),
                pltpu.VMEM((ITERS - 1, 2, side, side), f32),
                pltpu.VMEM((ITERS, 2, side, side), bf16),
                pltpu.VMEM((ITERS, 2, side, side), bf16),
                pltpu.VMEM((ITERS, 2, side, side), bf16),
                pltpu.VMEM((ITERS, 4, 2, side), f32),
                pltpu.VMEM((ITERS, 4, 2, side), f32),
                dma((12,)), dma((12,)),
                dma((3,)), dma((3,)),
                dma((9,)), dma((9,)),
                dma((3,)), dma((3,)), dma((4,)),
                dma((6,)), dma((6,)),
                dma((plane,)), dma((plane,)),
                dma((3,)), dma((3,)),
                dma((ITERS, 8)), dma((ITERS, 8)),
                dma((5,)),
            ],
            compiler_params=pltpu.CompilerParams(
                collective_id=0, has_side_effects=True, vmem_limit_bytes=56 * 1024 * 1024
            ),
        )(blocks, count, desc, pos, ids, disp, stiff)
        return moved[None]

    in_specs = (
        P("sec", "ty", "tx", None, None),
        P("sec", "ty", "tx", None, None),
        P("sec", "ty", "tx", None),
        P("sec", "ty", "tx", None),
        P("sec", "ty", "tx"),
        P("sec", None, "ty", "tx"),
        P("sec", "ty", "tx"),
    )
    return jax.shard_map(
        per_device, mesh=mesh, in_specs=in_specs, out_specs=P("sec", None, "ty", "tx"), check_vma=False
    )
```

```python
import functools
import math

import jax
import jax.numpy as jnp
from jax import lax
from jax.experimental import pallas as pl
from jax.experimental.pallas import tpu as pltpu
from jax.sharding import PartitionSpec as P

MESH = pl.DeviceIdType.MESH
BLK = 128
CAPB = 4
CHUNK = 256
ITERS = 4
NEG = -1e30
SPRING_SEC = 0.5
RATE = 0.8
NT = (((1,), (1,)), ((), ()))
NN = (((1,), (0,)), ((), ()))


def remote(src, dst, send, recv, device):
    return pltpu.make_async_remote_copy(
        src_ref=src, dst_ref=dst, send_sem=send, recv_sem=recv, device_id=device, device_id_type=MESH
    )


def block_table(list_ref, count_ref, slots):
    lane = lax.broadcasted_iota(jnp.int32, (8, 128), 1)
    row = lax.broadcasted_iota(jnp.int32, (8, 128), 0)
    within = lane & 7
    wanted = jnp.zeros((8, 128), jnp.int32)
    for entry in range(slots):
        block = jnp.where(count_ref[0, 0, 0] > entry, list_ref[entry], -1)
        wanted = jnp.where(lane == block, 1, wanted)
    rank = jnp.zeros((8, 128), jnp.int32)
    for by in range(1, 8):
        rank = rank + jnp.where(within >= by, pltpu.roll(wanted, by, 1), 0)
    picked = jnp.where((wanted == 1) & (rank == row), within + 1, 0)
    total = picked
    for by in range(1, 8):
        total = total + pltpu.roll(picked, 128 - by, 1)
    return jnp.where(total == 0, 8, total - 1)


def kernel(
    sizes, list_ref, count_ref, desc, pos, ids, disp, stiff, out,
    dispv, stiffv, posv, qbuf, kin0, kin1, kin2, kin3, pin, kwork, vwork, tabv, tabs, idb, onea, onec, mcount,
    acc, mx, sbuf0, sbuf1, tops0, tops1, part, prt, pull, pbuf, scat, coef, base, force, ub, first_below, first_above, wire, lob, upb, edge, halo,
    qs, qr, hs, hr, ks, kr, ts, tr, tl, ids_s, ids_r, ps, pr, cs, cr, us, ur, ls,
):
    ns, ny, nz, slots = sizes
    plane = ny * nz
    pts, feat = desc.shape
    half = pts // 2
    blocks = pts // BLK
    side = stiff.shape[0]
    s, y, z = lax.axis_index("sec"), lax.axis_index("ty"), lax.axis_index("tx")
    me = y * nz + z
    right, left = {"tx": lax.rem(z + 1, nz)}, {"tx": lax.rem(z + nz - 1, nz)}
    across = {"tx": lax.rem(z + 2, nz)}
    down, up = {"ty": lax.rem(y + 1, ny)}, {"ty": lax.rem(y + ny - 1, ny)}
    after, before = {"sec": lax.rem(s + 1, ns)}, {"sec": lax.rem(s + ns - 1, ns)}

    def peer(by):
        tile = lax.rem(me + by, plane)
        return tile, {"ty": lax.div(tile, nz), "tx": lax.rem(tile, nz)}

    barrier = pltpu.get_barrier_semaphore()

    near = (right, left, down, up, after, before)
    for device in near:
        pl.semaphore_signal(barrier, inc=1, device_id=device, device_id_type=MESH)
    loads = [
        pltpu.make_async_copy(desc, qbuf.at[0], ls.at[0]),
        pltpu.make_async_copy(pos, posv, ls.at[1]),
        pltpu.make_async_copy(ids, idb.at[me], ls.at[2]),
        pltpu.make_async_copy(disp, dispv, ls.at[3]),
        pltpu.make_async_copy(stiff, stiffv, ls.at[4]),
    ]
    for copy in loads:
        copy.start()

    tabv[0] = block_table(list_ref, count_ref, slots)
    acc[...] = jnp.zeros_like(acc)
    mx[...] = jnp.full_like(mx, NEG)
    mcount[...] = jnp.zeros_like(mcount)
    scat[...] = jnp.zeros_like(scat)

    pl.semaphore_wait(barrier, len(near))

    rows = [pl.ds(0, half), pl.ds(half, half)]
    shift = [
        remote(desc.at[rows[0]], kin0.at[rows[0]], hs.at[0], hr.at[0], before),
        remote(desc.at[rows[1]], kin0.at[rows[1]], hs.at[1], hr.at[1], before),
        remote(pos, pin.at[0], hs.at[2], hr.at[2], before),
    ]
    tables = [
        remote(tabv.at[0], tabv.at[1], ts.at[0], tr.at[0], right),
        remote(tabv.at[0], tabv.at[2], ts.at[1], tr.at[1], left),
        remote(tabv.at[1], tabv.at[3], ts.at[2], tr.at[2], right),
    ]
    piece = [pl.ds(at * CHUNK, CHUNK) for at in range(pts // CHUNK)]
    to_right = [remote(desc.at[piece[at]], qbuf.at[1, piece[at]], qs.at[at], qr.at[at], right) for at in range(4)]
    to_left = [
        remote(desc.at[piece[at]], qbuf.at[2, piece[at]], qs.at[4 + at], qr.at[4 + at], left)
        for at in (2, 3, 0, 1)
    ]
    on_right = [
        remote(qbuf.at[1, piece[at]], qbuf.at[3, piece[at]], qs.at[8 + at], qr.at[8 + at], right) for at in (0, 1)
    ]
    on_left = [
        remote(qbuf.at[2, piece[at]], qbuf.at[3, piece[at]], qs.at[8 + at], qr.at[8 + at], left) for at in (2, 3)
    ]
    queries = to_right + to_left + on_right + on_left
    lefts = y * nz + lax.rem(z + nz - 1, nz)
    row, row_up = pl.ds(y * nz, nz), pl.ds(lax.rem(y + ny - 1, ny) * nz, nz)
    names = [
        remote(ids, idb.at[me], ids_s.at[0], ids_r.at[0], right),
        remote(ids, idb.at[me], ids_s.at[1], ids_r.at[1], left),
        remote(idb.at[lefts], idb.at[lefts], ids_s.at[2], ids_r.at[2], right),
        remote(idb.at[row], idb.at[row], ids_s.at[3], ids_r.at[3], down),
        remote(idb.at[row], idb.at[row], ids_s.at[4], ids_r.at[4], up),
        remote(idb.at[row_up], idb.at[row_up], ids_s.at[5], ids_r.at[5], down),
    ]
    keys = [
        remote(kin0.at[rows[0]], kin1.at[rows[0]], ks.at[0], kr.at[0], down),
        remote(kin0.at[rows[1]], kin2.at[rows[1]], ks.at[1], kr.at[1], up),
        remote(kin0.at[rows[1]], kin1.at[rows[1]], ks.at[2], kr.at[2], down),
        remote(kin0.at[rows[0]], kin2.at[rows[0]], ks.at[3], kr.at[3], up),
        remote(kin1.at[rows[0]], kin3.at[rows[0]], ks.at[4], kr.at[4], down),
        remote(kin2.at[rows[1]], kin3.at[rows[1]], ks.at[5], kr.at[5], up),
        remote(pin.at[0], pin.at[1], ks.at[6], kr.at[6], down),
        remote(pin.at[0], pin.at[2], ks.at[7], kr.at[7], up),
        remote(pin.at[1], pin.at[3], ks.at[8], kr.at[8], down),
    ]
    partials = [
        remote(part.at[1], prt.at[2], cs.at[0], cr.at[0], left),
        remote(part.at[2], prt.at[1], cs.at[1], cr.at[1], right),
        remote(part.at[3], prt.at[3], cs.at[2], cr.at[2], across),
    ]

    def exchange(turn):
        if turn == 0:
            source, below, above = (
                [ref.at[channel] for channel in range(2)] for ref in (dispv, first_below, first_above)
            )
        else:
            source, below, above = (
                [ref.at[turn - 1, channel] for channel in range(2)] for ref in (wire, lob, upb)
            )
        return [
            remote(edge.at[turn, 0], halo.at[turn, 1], us.at[turn, 0], ur.at[turn, 0], up),
            remote(edge.at[turn, 1], halo.at[turn, 0], us.at[turn, 1], ur.at[turn, 1], down),
            remote(edge.at[turn, 2], halo.at[turn, 3], us.at[turn, 2], ur.at[turn, 2], left),
            remote(edge.at[turn, 3], halo.at[turn, 2], us.at[turn, 3], ur.at[turn, 3], right),
            remote(source[0], below[0], us.at[turn, 4], ur.at[turn, 4], after),
            remote(source[0], above[0], us.at[turn, 5], ur.at[turn, 5], before),
            remote(source[1], below[1], us.at[turn, 6], ur.at[turn, 6], after),
            remote(source[1], above[1], us.at[turn, 7], ur.at[turn, 7], before),
        ]

    swaps = [exchange(turn) for turn in range(ITERS)]

    def pull_copy(by):
        _, device = peer(by)
        return remote(pull, pbuf.at[me], ps.at[by], pr.at[me], device)

    def pull_from(tile):
        return remote(pull, pbuf.at[tile], ps.at[0], pr.at[tile], before)

    for copy in shift + tables[:2] + names[:2]:
        copy.start()
    for at in range(3):
        to_right[at].start()
        to_left[at].start()
    for copy in loads:
        copy.wait()

    def set_key(slot, source):
        kwork[slot] = source[...].reshape(blocks, BLK, feat)
        place = pin[slot].astype(jnp.float32)
        line = lax.broadcasted_iota(jnp.int32, (16, pts), 0)
        value = jnp.where(line == 2, 1.0, 0.0)
        value = jnp.where(line == 1, place[1:2], value)
        value = jnp.where(line == 0, place[0:1], value).astype(jnp.bfloat16)
        for block in range(blocks):
            vwork[slot, block] = value[:, block * BLK : (block + 1) * BLK]

    eye = lax.broadcasted_iota(jnp.int32, (side, side), 0) == lax.broadcasted_iota(jnp.int32, (side, side), 1)

    def set_edges(turn, channel, value):
        edge[turn, 0, channel : channel + 1, :] = value[0:1, :]
        edge[turn, 1, channel : channel + 1, :] = value[side - 1 : side, :]
        for at, column in ((2, value[:, 0:1]), (3, value[:, side - 1 : side])):
            spread = jnp.where(eye, jnp.broadcast_to(column, (side, side)), 0.0)
            edge[turn, at, channel : channel + 1, :] = jnp.sum(spread, axis=0, keepdims=True)

    for channel in range(2):
        set_edges(0, channel, dispv[channel])

    order = [(0, 0), (1, 0), (3, 0), (2, 0), (0, 1), (0, 3), (1, 1), (3, 1), (1, 3), (3, 3)]
    order += [(2, 1), (2, 3), (0, 2), (1, 2), (3, 2), (2, 2)]
    wrap = lambda value: value - (1 << 32) if value >= 1 << 31 else value
    code_y = wrap(sum(dy << (2 * at) for at, (dy, _) in enumerate(order)))
    code_z = wrap(sum(dz << (2 * at) for at, (_, dz) in enumerate(order)))

    def nearest(turn):
        ahead_y = (jnp.int32(code_y) >> (2 * turn)) & 3
        ahead_z = (jnp.int32(code_z) >> (2 * turn)) & 3
        return lax.rem(y + ahead_y, ny) * nz + lax.rem(z + ahead_z, nz)

    def one_hots(turn, carry):
        tile = nearest(turn)

        vertex = idb[tile]
        level = lax.broadcasted_iota(jnp.int32, (side, pts), 0)
        pick_row = level == ((vertex - me * (side * side)) >> 7)
        pick_col = level == (vertex & (side - 1))
        row_hot = jnp.where(pick_row, 1.0, 0.0).astype(jnp.bfloat16)
        col_hot = jnp.where(pick_col, 1.0, 0.0).astype(jnp.bfloat16)
        onea[tile] = row_hot
        onec[tile] = col_hot
        mcount[...] += lax.dot_general(row_hot, col_hot, NT, preferred_element_type=jnp.float32)
        return carry

    factor = 16.0 / feat * math.log2(math.e)

    def packed(values, at):
        return (jnp.int32(sum(value << (2 * i) for i, value in enumerate(values))) >> (2 * at)) & 3

    def unit(step):
        early = step < 8
        high, low = lax.div(step, 2), lax.rem(step, 2)
        parts = []
        for i in range(2):
            pair, k = jnp.where(early, 2 * low + i, high), jnp.where(early, high, 2 * low + i)
            for slots, places in (
                ((0, 0, 1, 1, 1, 3, 3, 1), (0, 2, 0, 1, 2, 0, 1, 3)),
                ((0, 0, 2, 2, 2, 3, 3, 2), (1, 3, 2, 3, 0, 2, 3, 1)),
            ):
                q = packed(slots, pair)
                start = pl.multiple_of(packed(places, pair) * CHUNK, CHUNK)
                key_row = lax.rem(y + packed((0, ny - 1, 1, 2), k), ny)
                lane = (key_row * nz + z) * 8
                codes = [tabs[q, slot, lane] for slot in range(CAPB)]
                found = [code & (blocks - 1) for code in codes]
                parts.append((q, k, pl.ds(start, CHUNK), found, [code < blocks for code in codes]))
        return parts

    def score(part_at, sbuf, tops, at):
        q, k, cols, at_block, live = part_at
        key_rows = jnp.concatenate([kwork[k, block] for block in at_block], axis=0)
        raw = lax.dot_general(key_rows, qbuf[q, cols, :], NT, preferred_element_type=jnp.float32)
        sbuf[at] = raw
        for i in range(CAPB):
            top = jnp.max(raw[i * BLK : (i + 1) * BLK], axis=0, keepdims=True)
            tops[at, i] = jnp.where(live[i], top, NEG)

    def weigh(part_at, sbuf, tops, at):
        q, k, cols, at_block, live = part_at
        values = jnp.concatenate([vwork[k, block] for block in at_block], axis=1)
        old = mx[q, :, cols]
        new = functools.reduce(jnp.maximum, [tops[at, i] for i in range(CAPB)], old)
        weights = []
        for i in range(CAPB):
            base = jnp.where(live[i], new, -NEG)
            raw = sbuf[at, i * BLK : (i + 1) * BLK, :]
            weights.append(jnp.exp2((raw - base) * factor).astype(jnp.bfloat16))
        added = lax.dot_general(values, jnp.concatenate(weights, axis=0), NN, preferred_element_type=jnp.float32)
        acc[q, :, cols] = acc[q, :, cols] * jnp.exp2((old - new) * factor) + added
        mx[q, :, cols] = new

    def load_table(slot):
        local = pltpu.make_async_copy(tabv.at[slot], tabs.at[slot], tl.at[slot])
        local.start()
        local.wait()

    def settle(slot):
        part[slot, 0:3, :] = acc[slot, 0:3, :]
        part[slot, 3:4, :] = mx[slot]

    def match(step, carry):
        @pl.when(step == 0)
        def _():
            keys[0].wait_recv()
            keys[4].start()
            keys[1].wait_recv()
            keys[5].start()
            keys[6].wait_recv()
            keys[8].start()
            to_right[0].wait_recv()
            on_right[0].start()
            to_left[0].wait_recv()
            on_left[0].start()
            for slot in (1, 2):
                tables[slot - 1].wait_recv()
                load_table(slot)
            tables[2].start()
            names[0].wait_recv()
            names[2].start()

            to_right[1].wait_recv()
            on_right[1].start()
            to_left[1].wait_recv()
            on_left[1].start()
            to_right[3].start()
            to_left[3].start()

        @pl.when(step == 1)
        def _():
            keys[2].wait_recv()
            set_key(1, kin1)

        @pl.when(step == 3)
        def _():
            keys[3].wait_recv()
            keys[7].wait_recv()
            set_key(2, kin2)

        @pl.when(step == 5)
        def _():
            keys[4].wait_recv()
            keys[5].wait_recv()
            keys[8].wait_recv()
            set_key(3, kin3)

        @pl.when(step == 7)
        def _():
            to_right[2].wait_recv()
            to_left[2].wait_recv()
            names[1].wait_recv()
            names[2].wait_recv()
            names[3].start()
            names[4].start()

        @pl.when(step == 9)
        def _():
            on_right[0].wait_recv()
            on_left[0].wait_recv()
            tables[2].wait_recv()
            load_table(3)

        @pl.when(step == 11)
        def _():
            on_right[1].wait_recv()
            on_left[1].wait_recv()
            names[3].wait_recv()
            names[5].start()
            for copy in swaps[0]:
                copy.start()

        @pl.when(step == 13)
        def _():
            to_right[3].wait_recv()
            to_left[3].wait_recv()

        for parity, first, second in ((0, (sbuf0, tops0), (sbuf1, tops1)), (1, (sbuf1, tops1), (sbuf0, tops0))):

            @pl.when(lax.rem(step, 2) == parity)
            def _():
                ahead, here = unit(step + 1), unit(step)
                for at in range(4):
                    score(ahead[at], *second, at)
                for at in range(4):
                    weigh(here[at], *first, at)

        @pl.when(step == 13)
        def _():
            settle(3)
            partials[2].start()

        return carry

    local = pltpu.make_async_copy(tabv.at[0], tabs.at[0], tl.at[0])
    local.start()
    local.wait()
    shift[0].wait_recv()
    keys[0].start()
    shift[1].wait_recv()
    keys[1].start()
    keys[2].start()
    keys[3].start()
    shift[2].wait_recv()
    keys[6].start()
    keys[7].start()
    set_key(0, kin0)
    for at, part_at in enumerate(unit(jnp.int32(0))):
        score(part_at, sbuf0, tops0, at)
    lax.fori_loop(0, 15, match, 0)
    for at, part_at in enumerate(unit(jnp.int32(15))):
        weigh(part_at, sbuf1, tops1, at)
    for slot in (1, 2):
        settle(slot)
        partials[slot - 1].start()
    settle(0)
    names[4].wait_recv()
    names[5].wait_recv()
    lax.fori_loop(0, plane // 2, one_hots, 0)

    has_next = s < ns - 1
    for copy in partials:
        copy.wait_recv()
    pieces = [part[0]] + [prt[slot] for slot in range(1, 4)]
    top = functools.reduce(jnp.maximum, [piece[3:4] for piece in pieces])
    scaled = [piece[0:3] * jnp.exp2((piece[3:4] - top) * factor) for piece in pieces]
    total = functools.reduce(jnp.add, scaled)
    mine = posv[...].astype(jnp.float32)
    pull[...] = jnp.where(has_next, total[0:2] / total[2:3] - mine, 0.0)

    def start_pull(by, carry):
        pull_copy(by).start()
        return carry

    lax.fori_loop(1, plane, start_pull, 0)
    pbuf[pl.ds(me, 1)] = pull[...][None]
    lax.fori_loop(plane // 2, plane, one_hots, 0)

    flag = lambda test: jnp.where(test, 1.0, 0.0)
    next_flag, last_flag = flag(s < ns - 1), flag(s > 0)
    row_at = lax.broadcasted_iota(jnp.int32, (side, side), 0)
    col_at = lax.broadcasted_iota(jnp.int32, (side, side), 1)
    flags = [flag(y > 0), flag(y < ny - 1), flag(z > 0), flag(z < nz - 1)]
    coef[0] = RATE / (4.0 * stiffv[...] + SPRING_SEC * (next_flag + last_flag) + mcount[...] * next_flag)
    coef[1] = coef[0] * stiffv[...]

    def inside(value):
        around = jnp.where(row_at == 0, 0.0, pltpu.roll(value, 1, 0))
        around += jnp.where(row_at == side - 1, 0.0, pltpu.roll(value, side - 1, 0))
        around += jnp.where(col_at == 0, 0.0, pltpu.roll(value, 1, 1))
        around += jnp.where(col_at == side - 1, 0.0, pltpu.roll(value, side - 1, 1))
        return (1.0 - RATE) * value + coef[1] * around

    def outside(turn, channel):
        lines = [halo[turn, at, channel : channel + 1, :] * flags[at] for at in range(4)]
        cols = [
            jnp.sum(jnp.where(eye, jnp.broadcast_to(line, (side, side)), 0.0), axis=1, keepdims=True)
            for line in lines[2:]
        ]
        edges = jnp.where(row_at == 0, lines[0], 0.0) + jnp.where(row_at == side - 1, lines[1], 0.0)
        edges += jnp.where(col_at == 0, cols[0], 0.0) + jnp.where(col_at == side - 1, cols[1], 0.0)
        below = first_below[channel] if turn == 0 else lob[turn - 1, channel].astype(jnp.float32)
        above = first_above[channel] if turn == 0 else upb[turn - 1, channel].astype(jnp.float32)
        stack = below * (SPRING_SEC * last_flag) + above * (SPRING_SEC * next_flag)
        return coef[1] * edges + coef[0] * stack

    for copy in swaps[0]:
        copy.wait_recv()
    for channel in range(2):
        base[channel] = inside(dispv[channel]) + outside(0, channel)

    def gather_pull(turn, carry):
        tile = nearest(turn)

        @pl.when(turn > 0)
        def _():
            pull_from(tile).wait_recv()

        row_hot = onea[tile].reshape(side // 16, 16, pts)
        pieces = []
        for channel in range(2):
            value = jnp.broadcast_to(pbuf[tile, channel : channel + 1, :], (16, pts)).astype(jnp.bfloat16)
            pieces.append((row_hot * value[None]).reshape(side, pts))
        stacked = jnp.concatenate(pieces, axis=0)
        scat[...] += lax.dot_general(stacked, onec[tile], NT, preferred_element_type=jnp.float32)
        return carry

    lax.fori_loop(0, plane, gather_pull, 0)

    pulled = [scat[0:side], scat[side:]]
    for channel in range(2):
        force[channel] = coef[0] * pulled[channel]
    for turn in range(ITERS):
        settled = []
        for channel in range(2):
            if turn == 0:
                settled.append(base[channel])
            else:
                settled.append(inside(ub[turn - 1, channel]) + force[channel])
        if turn > 0:
            for copy in swaps[turn]:
                copy.wait_recv()
        for channel in range(2):
            if turn == 0:
                moved = base[channel] + force[channel]
            else:
                moved = settled[channel] + outside(turn, channel)
            if turn == ITERS - 1:
                out[channel] = moved
            else:
                wire[turn, channel] = moved.astype(jnp.bfloat16)
                for copy in swaps[turn + 1][4 + 2 * channel : 6 + 2 * channel]:
                    copy.start()
                ub[turn, channel] = moved
                set_edges(turn + 1, channel, moved)
        if turn < ITERS - 1:
            for copy in swaps[turn + 1][:4]:
                copy.start()

    for copy in shift + tables + names + queries + keys + partials + [c for swap in swaps for c in swap]:
        copy.wait_send()

    def finish(by, carry):
        pull_copy(by).wait_send()
        return carry

    lax.fori_loop(1, plane, finish, 0)


def solution(mesh):
    ns, ny, nz = mesh.shape["sec"], mesh.shape["ty"], mesh.shape["tx"]

    def per_device(desc, pos, ids, blocks, count, disp, stiff):
        desc, pos, ids = desc[0, 0, 0], pos[0, 0, 0], ids[0, 0]
        blocks = blocks[0, 0, 0]
        disp, stiff = disp[0], stiff[0]
        pts, feat = desc.shape
        side = stiff.shape[0]
        plane = ny * nz
        bf16, f32, i32 = jnp.bfloat16, jnp.float32, jnp.int32
        tile = pltpu.VMEM((pts, feat), bf16)
        dma = pltpu.SemaphoreType.DMA
        smem = pl.BlockSpec(memory_space=pltpu.SMEM)
        vmem = pl.BlockSpec(memory_space=pltpu.VMEM)
        moved = pl.pallas_call(
            functools.partial(kernel, (ns, ny, nz, blocks.shape[0])),
            out_shape=jax.ShapeDtypeStruct(disp.shape, f32),
            in_specs=[smem, smem] + [pl.BlockSpec(memory_space=pl.ANY)] * 5,
            out_specs=vmem,
            scratch_shapes=[
                pltpu.VMEM((2, side, side), f32),
                pltpu.VMEM((side, side), f32),
                pltpu.VMEM((2, pts), bf16),
                pltpu.VMEM((4, pts, feat), bf16),
                tile, tile, tile, tile,
                pltpu.VMEM((4, 2, pts), bf16),
                pltpu.VMEM((4, pts // BLK, BLK, feat), bf16),
                pltpu.VMEM((4, pts // BLK, 16, BLK), bf16),
                pltpu.VMEM((4, 8, 128), i32),
                pltpu.SMEM((4, 8, 128), i32),
                pltpu.VMEM((plane, 1, pts), i32),
                pltpu.VMEM((plane, side, pts), bf16),
                pltpu.VMEM((plane, side, pts), bf16),
                pltpu.VMEM((side, side), f32),
                pltpu.VMEM((4, 16, pts), f32),
                pltpu.VMEM((4, 1, pts), f32),
                pltpu.VMEM((4, CAPB * BLK, CHUNK), f32),
                pltpu.VMEM((4, CAPB * BLK, CHUNK), f32),
                pltpu.VMEM((4, CAPB, 1, CHUNK), f32),
                pltpu.VMEM((4, CAPB, 1, CHUNK), f32),
                pltpu.VMEM((4, 4, pts), f32),
                pltpu.VMEM((4, 4, pts), f32),
                pltpu.VMEM((2, pts), f32),
                pltpu.VMEM((plane, 2, pts), f32),
                pltpu.VMEM((2 * side, side), f32),
                pltpu.VMEM((2, side, side), f32),
                pltpu.VMEM((2, side, side), f32),
                pltpu.VMEM((2, side, side), f32),
                pltpu.VMEM((ITERS - 1, 2, side, side), f32),
                pltpu.VMEM((2, side, side), f32),
                pltpu.VMEM((2, side, side), f32),
                pltpu.VMEM((ITERS - 1, 2, side, side), bf16),
                pltpu.VMEM((ITERS - 1, 2, side, side), bf16),
                pltpu.VMEM((ITERS - 1, 2, side, side), bf16),
                pltpu.VMEM((ITERS, 4, 2, side), f32),
                pltpu.VMEM((ITERS, 4, 2, side), f32),
                dma((12,)), dma((12,)),
                dma((3,)), dma((3,)),
                dma((9,)), dma((9,)),
                dma((3,)), dma((3,)), dma((4,)),
                dma((6,)), dma((6,)),
                dma((plane,)), dma((plane,)),
                dma((3,)), dma((3,)),
                dma((ITERS, 8)), dma((ITERS, 8)),
                dma((5,)),
            ],
            compiler_params=pltpu.CompilerParams(
                collective_id=0, has_side_effects=True, vmem_limit_bytes=56 * 1024 * 1024
            ),
        )(blocks, count, desc, pos, ids, disp, stiff)
        return moved[None]

    in_specs = (
        P("sec", "ty", "tx", None, None),
        P("sec", "ty", "tx", None, None),
        P("sec", "ty", "tx", None),
        P("sec", "ty", "tx", None),
        P("sec", "ty", "tx"),
        P("sec", None, "ty", "tx"),
        P("sec", "ty", "tx"),
    )
    return jax.shard_map(
        per_device, mesh=mesh, in_specs=in_specs, out_specs=P("sec", None, "ty", "tx"), check_vma=False
    )
```

```python
import functools
import math

import jax
import jax.numpy as jnp
from jax import lax
from jax.experimental import pallas as pl
from jax.experimental.pallas import tpu as pltpu
from jax.sharding import PartitionSpec as P

MESH = pl.DeviceIdType.MESH
BLK = 128
CAPB = 4
CHUNK = 256
ITERS = 4
NEG = -1e30
SPRING_SEC = 0.5
RATE = 0.8
NT = (((1,), (1,)), ((), ()))
NN = (((1,), (0,)), ((), ()))


def remote(src, dst, send, recv, device):
    return pltpu.make_async_remote_copy(
        src_ref=src, dst_ref=dst, send_sem=send, recv_sem=recv, device_id=device, device_id_type=MESH
    )


def block_table(list_ref, count_ref, slots):
    lane = lax.broadcasted_iota(jnp.int32, (8, 128), 1)
    row = lax.broadcasted_iota(jnp.int32, (8, 128), 0)
    within = lane & 7
    wanted = jnp.zeros((8, 128), jnp.int32)
    for entry in range(slots):
        block = jnp.where(count_ref[0, 0, 0] > entry, list_ref[entry], -1)
        wanted = jnp.where(lane == block, 1, wanted)
    rank = jnp.zeros((8, 128), jnp.int32)
    for by in range(1, 8):
        rank = rank + jnp.where(within >= by, pltpu.roll(wanted, by, 1), 0)
    picked = jnp.where((wanted == 1) & (rank == row), within + 1, 0)
    total = picked
    for by in range(1, 8):
        total = total + pltpu.roll(picked, 128 - by, 1)
    return jnp.where(total == 0, 8, total - 1)


def kernel(
    sizes, list_ref, count_ref, desc, pos, ids, disp, stiff, out,
    dispv, stiffv, posv, qbuf, kin0, kin1, kin2, kin3, pin, kwork, vwork, tabv, tabs, idb, onea, onec, mcount,
    acc, mx, sbuf0, sbuf1, tops0, tops1, part, prt, pull, pbuf, scat, coef, base, force, ub, first_below, first_above, wire, lob, upb, edge, halo,
    qs, qr, hs, hr, ks, kr, ts, tr, tl, ids_s, ids_r, ps, pr, cs, cr, us, ur, ls,
):
    ns, ny, nz, slots = sizes
    plane = ny * nz
    pts, feat = desc.shape
    half = pts // 2
    blocks = pts // BLK
    side = stiff.shape[0]
    s, y, z = lax.axis_index("sec"), lax.axis_index("ty"), lax.axis_index("tx")
    me = y * nz + z
    right, left = {"tx": lax.rem(z + 1, nz)}, {"tx": lax.rem(z + nz - 1, nz)}
    across = {"tx": lax.rem(z + 2, nz)}
    down, up = {"ty": lax.rem(y + 1, ny)}, {"ty": lax.rem(y + ny - 1, ny)}
    after, before = {"sec": lax.rem(s + 1, ns)}, {"sec": lax.rem(s + ns - 1, ns)}

    def peer(by):
        tile = lax.rem(me + by, plane)
        return tile, {"ty": lax.div(tile, nz), "tx": lax.rem(tile, nz)}

    barrier = pltpu.get_barrier_semaphore()

    near = (right, left, down, up, after, before)
    for device in near:
        pl.semaphore_signal(barrier, inc=1, device_id=device, device_id_type=MESH)
    loads = [
        pltpu.make_async_copy(desc, qbuf.at[0], ls.at[0]),
        pltpu.make_async_copy(pos, posv, ls.at[1]),
        pltpu.make_async_copy(ids, idb.at[me], ls.at[2]),
        pltpu.make_async_copy(disp, dispv, ls.at[3]),
        pltpu.make_async_copy(stiff, stiffv, ls.at[4]),
    ]
    for copy in loads:
        copy.start()

    tabv[0] = block_table(list_ref, count_ref, slots)
    acc[...] = jnp.zeros_like(acc)
    mx[...] = jnp.full_like(mx, NEG)
    mcount[...] = jnp.zeros_like(mcount)
    scat[...] = jnp.zeros_like(scat)

    pl.semaphore_wait(barrier, len(near))

    rows = [pl.ds(0, half), pl.ds(half, half)]
    shift = [
        remote(desc.at[rows[0]], kin0.at[rows[0]], hs.at[0], hr.at[0], before),
        remote(desc.at[rows[1]], kin0.at[rows[1]], hs.at[1], hr.at[1], before),
        remote(pos, pin.at[0], hs.at[2], hr.at[2], before),
    ]
    tables = [
        remote(tabv.at[0], tabv.at[1], ts.at[0], tr.at[0], right),
        remote(tabv.at[0], tabv.at[2], ts.at[1], tr.at[1], left),
        remote(tabv.at[1], tabv.at[3], ts.at[2], tr.at[2], right),
    ]
    piece = [pl.ds(at * CHUNK, CHUNK) for at in range(pts // CHUNK)]
    to_right = [remote(desc.at[piece[at]], qbuf.at[1, piece[at]], qs.at[at], qr.at[at], right) for at in range(4)]
    to_left = [
        remote(desc.at[piece[at]], qbuf.at[2, piece[at]], qs.at[4 + at], qr.at[4 + at], left)
        for at in (2, 3, 0, 1)
    ]
    on_right = [
        remote(qbuf.at[1, piece[at]], qbuf.at[3, piece[at]], qs.at[8 + at], qr.at[8 + at], right) for at in (0, 1)
    ]
    on_left = [
        remote(qbuf.at[2, piece[at]], qbuf.at[3, piece[at]], qs.at[8 + at], qr.at[8 + at], left) for at in (2, 3)
    ]
    queries = to_right + to_left + on_right + on_left
    lefts = y * nz + lax.rem(z + nz - 1, nz)
    row, row_up = pl.ds(y * nz, nz), pl.ds(lax.rem(y + ny - 1, ny) * nz, nz)
    names = [
        remote(ids, idb.at[me], ids_s.at[0], ids_r.at[0], right),
        remote(ids, idb.at[me], ids_s.at[1], ids_r.at[1], left),
        remote(idb.at[lefts], idb.at[lefts], ids_s.at[2], ids_r.at[2], right),
        remote(idb.at[row], idb.at[row], ids_s.at[3], ids_r.at[3], down),
        remote(idb.at[row], idb.at[row], ids_s.at[4], ids_r.at[4], up),
        remote(idb.at[row_up], idb.at[row_up], ids_s.at[5], ids_r.at[5], down),
    ]
    keys = [
        remote(kin0.at[rows[0]], kin1.at[rows[0]], ks.at[0], kr.at[0], down),
        remote(kin0.at[rows[1]], kin2.at[rows[1]], ks.at[1], kr.at[1], up),
        remote(kin0.at[rows[1]], kin1.at[rows[1]], ks.at[2], kr.at[2], down),
        remote(kin0.at[rows[0]], kin2.at[rows[0]], ks.at[3], kr.at[3], up),
        remote(kin1.at[rows[0]], kin3.at[rows[0]], ks.at[4], kr.at[4], down),
        remote(kin2.at[rows[1]], kin3.at[rows[1]], ks.at[5], kr.at[5], up),
        remote(pin.at[0], pin.at[1], ks.at[6], kr.at[6], down),
        remote(pin.at[0], pin.at[2], ks.at[7], kr.at[7], up),
        remote(pin.at[1], pin.at[3], ks.at[8], kr.at[8], down),
    ]
    partials = [
        remote(part.at[1], prt.at[2], cs.at[0], cr.at[0], left),
        remote(part.at[2], prt.at[1], cs.at[1], cr.at[1], right),
        remote(part.at[3], prt.at[3], cs.at[2], cr.at[2], across),
    ]

    def exchange(turn):
        if turn == 0:
            source, below, above = (
                [ref.at[channel] for channel in range(2)] for ref in (dispv, first_below, first_above)
            )
        else:
            source, below, above = (
                [ref.at[turn - 1, channel] for channel in range(2)] for ref in (wire, lob, upb)
            )
        return [
            remote(edge.at[turn, 0], halo.at[turn, 1], us.at[turn, 0], ur.at[turn, 0], up),
            remote(edge.at[turn, 1], halo.at[turn, 0], us.at[turn, 1], ur.at[turn, 1], down),
            remote(edge.at[turn, 2], halo.at[turn, 3], us.at[turn, 2], ur.at[turn, 2], left),
            remote(edge.at[turn, 3], halo.at[turn, 2], us.at[turn, 3], ur.at[turn, 3], right),
            remote(source[0], below[0], us.at[turn, 4], ur.at[turn, 4], after),
            remote(source[0], above[0], us.at[turn, 5], ur.at[turn, 5], before),
            remote(source[1], below[1], us.at[turn, 6], ur.at[turn, 6], after),
            remote(source[1], above[1], us.at[turn, 7], ur.at[turn, 7], before),
        ]

    swaps = [exchange(turn) for turn in range(ITERS)]

    def pull_copy(by):
        _, device = peer(by)
        return remote(pull, pbuf.at[me], ps.at[by], pr.at[me], device)

    def pull_from(tile):
        return remote(pull, pbuf.at[tile], ps.at[0], pr.at[tile], before)

    for copy in shift + tables[:2] + names[:2]:
        copy.start()
    for at in range(3):
        to_right[at].start()
        to_left[at].start()
    for copy in loads:
        copy.wait()

    def set_key(slot, source):
        kwork[slot] = source[...].reshape(blocks, BLK, feat)
        place = pin[slot].astype(jnp.float32)
        line = lax.broadcasted_iota(jnp.int32, (16, pts), 0)
        value = jnp.where(line == 2, 1.0, 0.0)
        value = jnp.where(line == 1, place[1:2], value)
        value = jnp.where(line == 0, place[0:1], value).astype(jnp.bfloat16)
        for block in range(blocks):
            vwork[slot, block] = value[:, block * BLK : (block + 1) * BLK]

    eye = lax.broadcasted_iota(jnp.int32, (side, side), 0) == lax.broadcasted_iota(jnp.int32, (side, side), 1)

    def set_edges(turn, channel, value):
        edge[turn, 0, channel : channel + 1, :] = value[0:1, :]
        edge[turn, 1, channel : channel + 1, :] = value[side - 1 : side, :]
        for at, column in ((2, value[:, 0:1]), (3, value[:, side - 1 : side])):
            spread = jnp.where(eye, jnp.broadcast_to(column, (side, side)), 0.0)
            edge[turn, at, channel : channel + 1, :] = jnp.sum(spread, axis=0, keepdims=True)

    for channel in range(2):
        set_edges(0, channel, dispv[channel])

    order = [(0, 0), (1, 0), (3, 0), (2, 0), (0, 1), (0, 3), (1, 1), (3, 1), (1, 3), (3, 3)]
    order += [(2, 1), (2, 3), (0, 2), (1, 2), (3, 2), (2, 2)]
    wrap = lambda value: value - (1 << 32) if value >= 1 << 31 else value
    code_y = wrap(sum(dy << (2 * at) for at, (dy, _) in enumerate(order)))
    code_z = wrap(sum(dz << (2 * at) for at, (_, dz) in enumerate(order)))

    def nearest(turn):
        ahead_y = (jnp.int32(code_y) >> (2 * turn)) & 3
        ahead_z = (jnp.int32(code_z) >> (2 * turn)) & 3
        return lax.rem(y + ahead_y, ny) * nz + lax.rem(z + ahead_z, nz)

    count_up = lax.broadcasted_iota(jnp.int32, (16, pts), 0)
    levels = [(count_up + at).astype(jnp.float32).astype(jnp.bfloat16) for at in range(0, side, 16)]
    one, zero = jnp.ones((16, pts), jnp.bfloat16), jnp.zeros((16, pts), jnp.bfloat16)

    def one_hots(turn, carry):
        tile = nearest(turn)

        vertex = idb[tile]
        hots = []
        for place in ((vertex - me * (side * side)) >> 7, vertex & (side - 1)):
            spread = jnp.broadcast_to(place.astype(jnp.float32), (16, pts)).astype(jnp.bfloat16)
            hots.append(jnp.concatenate([jnp.where(level == spread, one, zero) for level in levels], axis=0))
        row_hot, col_hot = hots
        onea[tile] = row_hot
        onec[tile] = col_hot
        mcount[...] += lax.dot_general(row_hot, col_hot, NT, preferred_element_type=jnp.float32)
        return carry

    factor = 16.0 / feat * math.log2(math.e)

    def packed(values, at):
        return (jnp.int32(sum(value << (2 * i) for i, value in enumerate(values))) >> (2 * at)) & 3

    def unit(step):
        early = step < 8
        high, low = lax.div(step, 2), lax.rem(step, 2)
        parts = []
        for i in range(2):
            pair, k = jnp.where(early, 2 * low + i, high), jnp.where(early, high, 2 * low + i)
            for slots, places in (
                ((0, 0, 1, 1, 1, 3, 3, 1), (0, 2, 0, 1, 2, 0, 1, 3)),
                ((0, 0, 2, 2, 2, 3, 3, 2), (1, 3, 2, 3, 0, 2, 3, 1)),
            ):
                q = packed(slots, pair)
                start = pl.multiple_of(packed(places, pair) * CHUNK, CHUNK)
                key_row = lax.rem(y + packed((0, ny - 1, 1, 2), k), ny)
                lane = (key_row * nz + z) * 8
                codes = [tabs[q, slot, lane] for slot in range(CAPB)]
                found = [code & (blocks - 1) for code in codes]
                parts.append((q, k, pl.ds(start, CHUNK), found, [code < blocks for code in codes]))
        return parts

    def score(part_at, sbuf, tops, at):
        q, k, cols, at_block, live = part_at
        key_rows = jnp.concatenate([kwork[k, block] for block in at_block], axis=0)
        raw = lax.dot_general(key_rows, qbuf[q, cols, :], NT, preferred_element_type=jnp.float32)
        sbuf[at] = raw
        for i in range(CAPB):
            top = jnp.max(raw[i * BLK : (i + 1) * BLK], axis=0, keepdims=True)
            tops[at, i] = jnp.where(live[i], top, NEG)

    def weigh(part_at, sbuf, tops, at):
        q, k, cols, at_block, live = part_at
        values = jnp.concatenate([vwork[k, block] for block in at_block], axis=1)
        old = mx[q, :, cols]
        new = functools.reduce(jnp.maximum, [tops[at, i] for i in range(CAPB)], old)
        weights = []
        for i in range(CAPB):
            base = jnp.where(live[i], new, -NEG)
            raw = sbuf[at, i * BLK : (i + 1) * BLK, :]
            weights.append(jnp.exp2((raw - base) * factor).astype(jnp.bfloat16))
        added = lax.dot_general(values, jnp.concatenate(weights, axis=0), NN, preferred_element_type=jnp.float32)
        acc[q, :, cols] = acc[q, :, cols] * jnp.exp2((old - new) * factor) + added
        mx[q, :, cols] = new

    def load_table(slot):
        local = pltpu.make_async_copy(tabv.at[slot], tabs.at[slot], tl.at[slot])
        local.start()
        local.wait()

    def settle(slot):
        part[slot, 0:3, :] = acc[slot, 0:3, :]
        part[slot, 3:4, :] = mx[slot]

    def match(step, carry):
        @pl.when(step == 0)
        def _():
            keys[0].wait_recv()
            keys[4].start()
            keys[1].wait_recv()
            keys[5].start()
            keys[6].wait_recv()
            keys[8].start()
            to_right[0].wait_recv()
            on_right[0].start()
            to_left[0].wait_recv()
            on_left[0].start()
            for slot in (1, 2):
                tables[slot - 1].wait_recv()
                load_table(slot)
            tables[2].start()
            names[0].wait_recv()
            names[2].start()

            to_right[1].wait_recv()
            on_right[1].start()
            to_left[1].wait_recv()
            on_left[1].start()
            to_right[3].start()
            to_left[3].start()

        @pl.when(step == 1)
        def _():
            keys[2].wait_recv()
            set_key(1, kin1)

        @pl.when(step == 3)
        def _():
            keys[3].wait_recv()
            keys[7].wait_recv()
            set_key(2, kin2)

        @pl.when(step == 5)
        def _():
            keys[4].wait_recv()
            keys[5].wait_recv()
            keys[8].wait_recv()
            set_key(3, kin3)

        @pl.when(step == 7)
        def _():
            to_right[2].wait_recv()
            to_left[2].wait_recv()
            names[1].wait_recv()
            names[2].wait_recv()
            names[3].start()
            names[4].start()

        @pl.when(step == 9)
        def _():
            on_right[0].wait_recv()
            on_left[0].wait_recv()
            tables[2].wait_recv()
            load_table(3)

        @pl.when(step == 11)
        def _():
            on_right[1].wait_recv()
            on_left[1].wait_recv()
            names[3].wait_recv()
            names[5].start()
            for copy in swaps[0]:
                copy.start()

        @pl.when(step == 13)
        def _():
            to_right[3].wait_recv()
            to_left[3].wait_recv()

        for parity, first, second in ((0, (sbuf0, tops0), (sbuf1, tops1)), (1, (sbuf1, tops1), (sbuf0, tops0))):

            @pl.when(lax.rem(step, 2) == parity)
            def _():
                ahead, here = unit(step + 1), unit(step)
                for at in range(4):
                    score(ahead[at], *second, at)
                for at in range(4):
                    weigh(here[at], *first, at)

        @pl.when(step == 13)
        def _():
            settle(3)
            partials[2].start()

        return carry

    local = pltpu.make_async_copy(tabv.at[0], tabs.at[0], tl.at[0])
    local.start()
    local.wait()
    shift[0].wait_recv()
    keys[0].start()
    shift[1].wait_recv()
    keys[1].start()
    keys[2].start()
    keys[3].start()
    shift[2].wait_recv()
    keys[6].start()
    keys[7].start()
    set_key(0, kin0)
    for at, part_at in enumerate(unit(jnp.int32(0))):
        score(part_at, sbuf0, tops0, at)
    lax.fori_loop(0, 15, match, 0)
    for at, part_at in enumerate(unit(jnp.int32(15))):
        weigh(part_at, sbuf1, tops1, at)
    for slot in (1, 2):
        settle(slot)
        partials[slot - 1].start()
    settle(0)
    names[4].wait_recv()
    names[5].wait_recv()
    lax.fori_loop(0, plane // 2, one_hots, 0)

    has_next = s < ns - 1
    for copy in partials:
        copy.wait_recv()
    pieces = [part[0]] + [prt[slot] for slot in range(1, 4)]
    top = functools.reduce(jnp.maximum, [piece[3:4] for piece in pieces])
    scaled = [piece[0:3] * jnp.exp2((piece[3:4] - top) * factor) for piece in pieces]
    total = functools.reduce(jnp.add, scaled)
    mine = posv[...].astype(jnp.float32)
    pull[...] = jnp.where(has_next, total[0:2] / total[2:3] - mine, 0.0)

    def start_pull(by, carry):
        pull_copy(by).start()
        return carry

    lax.fori_loop(1, plane, start_pull, 0)
    pbuf[pl.ds(me, 1)] = pull[...][None]
    lax.fori_loop(plane // 2, plane, one_hots, 0)

    flag = lambda test: jnp.where(test, 1.0, 0.0)
    next_flag, last_flag = flag(s < ns - 1), flag(s > 0)
    row_at = lax.broadcasted_iota(jnp.int32, (side, side), 0)
    col_at = lax.broadcasted_iota(jnp.int32, (side, side), 1)
    flags = [flag(y > 0), flag(y < ny - 1), flag(z > 0), flag(z < nz - 1)]
    coef[0] = RATE / (4.0 * stiffv[...] + SPRING_SEC * (next_flag + last_flag) + mcount[...] * next_flag)
    coef[1] = coef[0] * stiffv[...]

    def inside(value):
        around = jnp.where(row_at == 0, 0.0, pltpu.roll(value, 1, 0))
        around += jnp.where(row_at == side - 1, 0.0, pltpu.roll(value, side - 1, 0))
        around += jnp.where(col_at == 0, 0.0, pltpu.roll(value, 1, 1))
        around += jnp.where(col_at == side - 1, 0.0, pltpu.roll(value, side - 1, 1))
        return (1.0 - RATE) * value + coef[1] * around

    def outside(turn, channel):
        lines = [halo[turn, at, channel : channel + 1, :] * flags[at] for at in range(4)]
        cols = [
            jnp.sum(jnp.where(eye, jnp.broadcast_to(line, (side, side)), 0.0), axis=1, keepdims=True)
            for line in lines[2:]
        ]
        edges = jnp.where(row_at == 0, lines[0], 0.0) + jnp.where(row_at == side - 1, lines[1], 0.0)
        edges += jnp.where(col_at == 0, cols[0], 0.0) + jnp.where(col_at == side - 1, cols[1], 0.0)
        below = first_below[channel] if turn == 0 else lob[turn - 1, channel].astype(jnp.float32)
        above = first_above[channel] if turn == 0 else upb[turn - 1, channel].astype(jnp.float32)
        stack = below * (SPRING_SEC * last_flag) + above * (SPRING_SEC * next_flag)
        return coef[1] * edges + coef[0] * stack

    for copy in swaps[0]:
        copy.wait_recv()
    for channel in range(2):
        base[channel] = inside(dispv[channel]) + outside(0, channel)

    def gather_pull(turn, carry):
        tile = nearest(turn)

        @pl.when(turn > 0)
        def _():
            pull_from(tile).wait_recv()

        row_hot = onea[tile].reshape(side // 16, 16, pts)
        pieces = []
        for channel in range(2):
            value = jnp.broadcast_to(pbuf[tile, channel : channel + 1, :], (16, pts)).astype(jnp.bfloat16)
            pieces.append((row_hot * value[None]).reshape(side, pts))
        stacked = jnp.concatenate(pieces, axis=0)
        scat[...] += lax.dot_general(stacked, onec[tile], NT, preferred_element_type=jnp.float32)
        return carry

    lax.fori_loop(0, plane, gather_pull, 0)

    pulled = [scat[0:side], scat[side:]]
    for channel in range(2):
        force[channel] = coef[0] * pulled[channel]
    for turn in range(ITERS):
        settled = []
        for channel in range(2):
            if turn == 0:
                settled.append(base[channel])
            else:
                settled.append(inside(ub[turn - 1, channel]) + force[channel])
        if turn > 0:
            for copy in swaps[turn]:
                copy.wait_recv()
        for channel in range(2):
            if turn == 0:
                moved = base[channel] + force[channel]
            else:
                moved = settled[channel] + outside(turn, channel)
            if turn == ITERS - 1:
                out[channel] = moved
            else:
                wire[turn, channel] = moved.astype(jnp.bfloat16)
                if channel == 0:
                    for copy in swaps[turn + 1][4:6]:
                        copy.start()
                ub[turn, channel] = moved
                set_edges(turn + 1, channel, moved)
        if turn < ITERS - 1:
            for copy in swaps[turn + 1][:4] + swaps[turn + 1][6:]:
                copy.start()

    for copy in shift + tables + names + queries + keys + partials + [c for swap in swaps for c in swap]:
        copy.wait_send()

    def finish(by, carry):
        pull_copy(by).wait_send()
        return carry

    lax.fori_loop(1, plane, finish, 0)


def solution(mesh):
    ns, ny, nz = mesh.shape["sec"], mesh.shape["ty"], mesh.shape["tx"]

    def per_device(desc, pos, ids, blocks, count, disp, stiff):
        desc, pos, ids = desc[0, 0, 0], pos[0, 0, 0], ids[0, 0]
        blocks = blocks[0, 0, 0]
        disp, stiff = disp[0], stiff[0]
        pts, feat = desc.shape
        side = stiff.shape[0]
        plane = ny * nz
        bf16, f32, i32 = jnp.bfloat16, jnp.float32, jnp.int32
        tile = pltpu.VMEM((pts, feat), bf16)
        dma = pltpu.SemaphoreType.DMA
        smem = pl.BlockSpec(memory_space=pltpu.SMEM)
        vmem = pl.BlockSpec(memory_space=pltpu.VMEM)
        moved = pl.pallas_call(
            functools.partial(kernel, (ns, ny, nz, blocks.shape[0])),
            out_shape=jax.ShapeDtypeStruct(disp.shape, f32),
            in_specs=[smem, smem] + [pl.BlockSpec(memory_space=pl.ANY)] * 5,
            out_specs=vmem,
            scratch_shapes=[
                pltpu.VMEM((2, side, side), f32),
                pltpu.VMEM((side, side), f32),
                pltpu.VMEM((2, pts), bf16),
                pltpu.VMEM((4, pts, feat), bf16),
                tile, tile, tile, tile,
                pltpu.VMEM((4, 2, pts), bf16),
                pltpu.VMEM((4, pts // BLK, BLK, feat), bf16),
                pltpu.VMEM((4, pts // BLK, 16, BLK), bf16),
                pltpu.VMEM((4, 8, 128), i32),
                pltpu.SMEM((4, 8, 128), i32),
                pltpu.VMEM((plane, 1, pts), i32),
                pltpu.VMEM((plane, side, pts), bf16),
                pltpu.VMEM((plane, side, pts), bf16),
                pltpu.VMEM((side, side), f32),
                pltpu.VMEM((4, 16, pts), f32),
                pltpu.VMEM((4, 1, pts), f32),
                pltpu.VMEM((4, CAPB * BLK, CHUNK), f32),
                pltpu.VMEM((4, CAPB * BLK, CHUNK), f32),
                pltpu.VMEM((4, CAPB, 1, CHUNK), f32),
                pltpu.VMEM((4, CAPB, 1, CHUNK), f32),
                pltpu.VMEM((4, 4, pts), f32),
                pltpu.VMEM((4, 4, pts), f32),
                pltpu.VMEM((2, pts), f32),
                pltpu.VMEM((plane, 2, pts), f32),
                pltpu.VMEM((2 * side, side), f32),
                pltpu.VMEM((2, side, side), f32),
                pltpu.VMEM((2, side, side), f32),
                pltpu.VMEM((2, side, side), f32),
                pltpu.VMEM((ITERS - 1, 2, side, side), f32),
                pltpu.VMEM((2, side, side), f32),
                pltpu.VMEM((2, side, side), f32),
                pltpu.VMEM((ITERS - 1, 2, side, side), bf16),
                pltpu.VMEM((ITERS - 1, 2, side, side), bf16),
                pltpu.VMEM((ITERS - 1, 2, side, side), bf16),
                pltpu.VMEM((ITERS, 4, 2, side), f32),
                pltpu.VMEM((ITERS, 4, 2, side), f32),
                dma((12,)), dma((12,)),
                dma((3,)), dma((3,)),
                dma((9,)), dma((9,)),
                dma((3,)), dma((3,)), dma((4,)),
                dma((6,)), dma((6,)),
                dma((plane,)), dma((plane,)),
                dma((3,)), dma((3,)),
                dma((ITERS, 8)), dma((ITERS, 8)),
                dma((5,)),
            ],
            compiler_params=pltpu.CompilerParams(
                collective_id=0, has_side_effects=True, vmem_limit_bytes=56 * 1024 * 1024
            ),
        )(blocks, count, desc, pos, ids, disp, stiff)
        return moved[None]

    in_specs = (
        P("sec", "ty", "tx", None, None),
        P("sec", "ty", "tx", None, None),
        P("sec", "ty", "tx", None),
        P("sec", "ty", "tx", None),
        P("sec", "ty", "tx"),
        P("sec", None, "ty", "tx"),
        P("sec", "ty", "tx"),
    )
    return jax.shard_map(
        per_device, mesh=mesh, in_specs=in_specs, out_specs=P("sec", None, "ty", "tx"), check_vma=False
    )
```
